32 devices in a mesh: section: 2 (over y), replica: 16 (over z, x, core).
Axes of the slice: x: 2, y: 2, z: 4, core: 2. Of those that a mesh axis runs over, the one named last changes fastest.
Arguments:
- coords_in: bfloat16 [2, 2048, 512], P(None, 'replica'), may hold values from -6 to 6
- token_rows: bfloat16 [2, 2048, 2048], P(None, 'replica'), may hold values from -6 to 6
- cotangent: bfloat16 [2, 2048, 512], P(None, 'replica'), may hold values from -6 to 6
- subspace_basis: bfloat16 [512, 2048], replicated, may hold values from -0.25 to 0.25
- norm_gain: float32 [2, 2048], P('section'), may hold values from 0.5 to 1.5
- gate_weight: float32 [2, 2048, 256], P('section', 'replica'), may hold values from -0.125 to 0.125
- up_weight: bfloat16 [2, 2048, 256], P('section', 'replica'), may hold values from -0.125 to 0.125
- down_weight: float32 [2, 256, 512], P('section', 'replica'), may hold values from -0.375 to 0.375
- gate_moment: float32 [2, 2048, 256], P('section', 'replica'), may hold values from -0.625 to 0.625
- gate_second: float32 [2, 2048, 256], P('section', 'replica'), may hold values from 0.01 to 0.1
- down_moment: float32 [2, 256, 512], P('section', 'replica'), may hold values from -0.625 to 0.625
- down_second: float32 [2, 256, 512], P('section', 'replica'), may hold values from 0.01 to 0.1
Outputs:
- section_coords: bfloat16 [2, 2, 2048, 512], P('section', None, 'replica')
- coord_grads: bfloat16 [2, 2, 2048, 512], P('section', None, 'replica')
- gate_new: float32 [2, 2048, 256], P('section', 'replica')
- gate_moment_new: float32 [2, 2048, 256], P('section', 'replica')
- gate_second_new: float32 [2, 2048, 256], P('section', 'replica')
- down_new: float32 [2, 256, 512], P('section', 'replica')
- down_moment_new: float32 [2, 256, 512], P('section', 'replica')
- down_second_new: float32 [2, 256, 512], P('section', 'replica')
The draws below stay inside these ranges and needn't reach their ends.
All inputs are finite; a program needn't handle non-finite values.
Results may differ from the reference program's by a relative error of at most 0.03.
Values may be sent and summed in bfloat16 or wider, within the bound.
No kernel may reach another device: no remote copies, remote signals or barrier semaphores. Data moves between devices by JAX's collectives and lax.ppermute only.
A program may use at most 64 MiB of HBM per device.

```python
import math
import jax
import jax.numpy as jnp
from jax import lax

D = 2048
FF = 256
K = 512
MB = 2
ROWS = 2048
TOKENS = 4096
SECTIONS = 2


def with_spikes(array, own_key, source, target, parts, factor):
    def block_of(axis_at):
        return (jnp.arange(array.shape[axis_at]) // (array.shape[axis_at] // parts)).reshape((-1,) + (1,) * (array.ndim - 1 - axis_at))

    first = jax.random.permutation(own_key, parts)[block_of(target)]
    far = (block_of(target) + parts // 2) % parts
    return jnp.where((block_of(source) == first) | (block_of(source) == far), factor * array, array)


def block_scale(rng, extent, cuts, smallest, top_value):
    level, own = 1.0, jax.random.fold_in(rng, 6)
    for position, parts in cuts:
        heights = jnp.exp(jax.random.uniform(jax.random.fold_in(own, position), (parts,), jnp.float32, smallest / len(cuts), top_value / len(cuts)))
        level = level * jnp.repeat(heights, extent[position] // parts).reshape([-1 if axis == position else 1 for axis in range(len(extent))])
    return level


def gaussian(rng, extent, deviation, most, pieces=(), held_as=jnp.bfloat16):
    factor_of = block_scale(rng, extent, pieces, -0.22, 0.18) if pieces else 1.0
    result = jax.random.normal(rng, extent, jnp.float32) * deviation * factor_of
    return jnp.minimum(jnp.maximum(result, -most), most).astype(held_as)


def gaussian_with(stream_key, dims, scale, limit, pieces, heavy, kind=jnp.bfloat16):
    entries = scale * jax.random.normal(stream_key, dims, jnp.float32)
    if pieces:
        entries = entries * block_scale(stream_key, dims, pieces, -0.22, 0.18)
    return jnp.clip(with_spikes(entries, jax.random.fold_in(stream_key, 3), *heavy), -limit, limit).astype(kind)


def setup_inputs(seed: int = 0) -> dict:
    splits = jax.random.split(jax.random.key(seed), 13)
    coords_in = gaussian(splits[0], (MB, ROWS, K), 1.0, 6.0, ((1, 16),))
    token_rows = gaussian_with(splits[1], (MB, ROWS, D), 1.0, 6.0, ((1, 16),), (1, 2, 16, 2.0))
    cotangent = gaussian(splits[2], (MB, ROWS, K), 1.0, 6.0, ((1, 16),))
    subspace_basis = gaussian(splits[3], (K, D), K ** -0.5, 0.25)
    norm_gain = jnp.clip(0.5 + 1.0 * jax.random.uniform(splits[4], (SECTIONS, D), jnp.float32) ** block_scale(splits[4], (SECTIONS, D), ((0, 2),), -0.2, 0.2), 0.5, 1.5)
    gate_weight = gaussian(splits[5], (SECTIONS, D, FF), D ** -0.5, 0.125, ((0, 2), (1, 16)), jnp.float32)
    up_weight = gaussian(splits[6], (SECTIONS, D, FF), D ** -0.5, 0.125, ((0, 2), (1, 16)))
    down_weight = gaussian(splits[7], (SECTIONS, FF, K), FF ** -0.5, 0.375, ((0, 2), (1, 16)), jnp.float32)
    gate_moment = gaussian(splits[8], (SECTIONS, D, FF), 0.1, 0.625, ((0, 2), (1, 16)), jnp.float32)
    gate_second = jnp.clip(jnp.exp(math.log(0.1) - 2.3025851 * jax.random.uniform(splits[9], (SECTIONS, D, FF), jnp.float32) ** block_scale(splits[9], (SECTIONS, D, FF), ((0, 2), (1, 16)), -0.2, 0.2)), 0.01, 0.1)
    down_moment = gaussian(splits[10], (SECTIONS, FF, K), 0.1, 0.625, ((0, 2), (1, 16)), jnp.float32)
    down_second = jnp.clip(jnp.exp(math.log(0.1) - 2.3025851 * jax.random.uniform(splits[11], (SECTIONS, FF, K), jnp.float32) ** block_scale(splits[11], (SECTIONS, FF, K), ((0, 2), (1, 16)), -0.2, 0.2)), 0.01, 0.1)
    return {"coords_in": coords_in, "token_rows": token_rows, "cotangent": cotangent, "subspace_basis": subspace_basis, "norm_gain": norm_gain, "gate_weight": gate_weight, "up_weight": up_weight, "down_weight": down_weight, "gate_moment": gate_moment, "gate_second": gate_second, "down_moment": down_moment, "down_second": down_second}


epsilon = 1e-06
learn_rate = 0.001
decay_first = 0.9
decay_second = 0.95
step_count = 10
adam_floor = 1e-08

def contract_last(left, right):
    return lax.dot_general(left, right, (((1,), (1,)), ((), ())), preferred_element_type=jnp.float32)

def contract_first(left, right):
    return lax.dot_general(left, right, (((0,), (0,)), ((), ())), preferred_element_type=jnp.float32)

def silu_parts(gate_value):
    sigma = jax.nn.sigmoid(gate_value)
    return (gate_value * sigma, sigma * (1.0 + gate_value * (1.0 - sigma)))

def section_forward(coords, token_block, subspace_basis, gain_row, w_gate, w_up, w_down):
    expanded = jnp.dot(coords, subspace_basis, preferred_element_type=jnp.float32) + token_block.astype(jnp.float32)
    inverse = lax.rsqrt(lax.optimization_barrier(jnp.mean(expanded * expanded, axis=1, keepdims=True)) + epsilon)
    normed = (expanded * inverse * gain_row).astype(jnp.bfloat16)
    gate_value = jnp.dot(normed, w_gate, preferred_element_type=jnp.float32)
    up_value = jnp.dot(normed, w_up, preferred_element_type=jnp.float32)
    active, slope_value = silu_parts(gate_value)
    hidden = (active * up_value).astype(jnp.bfloat16)
    output = (coords.astype(jnp.float32) + jnp.dot(hidden, w_down, preferred_element_type=jnp.float32)).astype(jnp.bfloat16)
    return (output, (expanded, inverse, normed, gate_value, up_value, hidden))

def section_backward(next_grad, saved, subspace_basis, gain_row, w_gate, w_up, w_down):
    expanded, inverse, normed, gate_value, up_value, hidden = saved
    hidden_grad = contract_last(next_grad, w_down)
    down_term = contract_first(hidden, next_grad)
    active, slope_value = silu_parts(gate_value)
    gate_grad = (hidden_grad * up_value * slope_value).astype(jnp.bfloat16)
    up_grad = (hidden_grad * active).astype(jnp.bfloat16)
    gate_term = contract_first(normed, gate_grad)
    normed_grad = contract_last(gate_grad, w_gate) + contract_last(up_grad, w_up)
    scaled = normed_grad * gain_row
    centred = expanded * inverse
    expanded_grad = (inverse * (scaled - centred * lax.optimization_barrier(jnp.mean(scaled * centred, axis=1, keepdims=True)))).astype(jnp.bfloat16)
    coord_grad = (next_grad.astype(jnp.float32) + contract_last(expanded_grad, subspace_basis)).astype(jnp.bfloat16)
    return (coord_grad, gate_term, down_term)

def adam_update(weight_now, moment, second, gradient):
    moment_new = decay_first * moment + (1.0 - decay_first) * gradient
    second_new = decay_second * second + (1.0 - decay_second) * gradient * gradient
    update = learn_rate * (moment_new / (1.0 - decay_first ** step_count)) / (jnp.sqrt(second_new / (1.0 - decay_second ** step_count)) + adam_floor)
    return (weight_now - update, moment_new, second_new)

def reference(coords_in, token_rows, cotangent, subspace_basis, norm_gain, gate_weight, up_weight, down_weight, gate_moment, gate_second, down_moment, down_second):
    gate_low = gate_weight.astype(jnp.bfloat16)
    down_low = down_weight.astype(jnp.bfloat16)
    layer_inputs = []
    layer_outputs = []
    current = coords_in
    for layer_index in range(SECTIONS):
        layer_inputs.append(current)
        weights = (subspace_basis, norm_gain[layer_index][None, :], gate_low[layer_index], up_weight[layer_index], down_low[layer_index])
        results = [section_forward(current[batch_index], token_rows[batch_index], *weights)[0] for batch_index in range(MB)]
        current = jnp.stack(results)
        layer_outputs.append(current)
    section_coords = jnp.stack(layer_outputs)
    grad_scale = 1.0 / math.sqrt(TOKENS)
    next_grads = cotangent
    back_list = [None] * SECTIONS
    gate_parts = [None] * SECTIONS
    down_parts = [None] * SECTIONS
    for layer_index in range(SECTIONS - 1, -1, -1):
        weights = (subspace_basis, norm_gain[layer_index][None, :], gate_low[layer_index], up_weight[layer_index], down_low[layer_index])
        coord_list = []
        gate_total = jnp.zeros((D, FF), jnp.float32)
        down_total = jnp.zeros((FF, K), jnp.float32)
        for batch_index in range(MB):
            saved = section_forward(layer_inputs[layer_index][batch_index], token_rows[batch_index], *weights)[1]
            coord_grad, gate_term, down_term = section_backward(next_grads[batch_index], saved, *weights)
            coord_list.append(coord_grad)
            gate_total = gate_total + gate_term
            down_total = down_total + down_term
        next_grads = jnp.stack(coord_list)
        back_list[layer_index] = next_grads
        gate_parts[layer_index] = adam_update(gate_weight[layer_index], gate_moment[layer_index], gate_second[layer_index], gate_total * grad_scale)
        down_parts[layer_index] = adam_update(down_weight[layer_index], down_moment[layer_index], down_second[layer_index], down_total * grad_scale)
    coord_grads = jnp.stack(back_list)
    gate_new = jnp.stack([item[0] for item in gate_parts])
    gate_moment_new = jnp.stack([item[1] for item in gate_parts])
    gate_second_new = jnp.stack([item[2] for item in gate_parts])
    down_new = jnp.stack([item[0] for item in down_parts])
    down_moment_new = jnp.stack([item[1] for item in down_parts])
    down_second_new = jnp.stack([item[2] for item in down_parts])
    return (section_coords, coord_grads, gate_new, gate_moment_new, gate_second_new, down_new, down_moment_new, down_second_new)
```

```python
import math

import jax
import jax.numpy as jnp
from jax import lax
from jax.sharding import PartitionSpec as P

epsilon = 1e-06
learn_rate = 0.001
decay_first = 0.9
decay_second = 0.95
step_count = 10
adam_floor = 1e-08


def contract_last(left, right):
    return lax.dot_general(
        left, right, (((1,), (1,)), ((), ())), preferred_element_type=jnp.float32
    )


def contract_first(left, right):
    return lax.dot_general(
        left, right, (((0,), (0,)), ((), ())), preferred_element_type=jnp.float32
    )


def shift(value, axis, steps):
    count = lax.axis_size(axis)
    first, last = max(0, -steps), min(count, count - steps)
    return lax.ppermute(value, axis, [(source, source + steps) for source in range(first, last)])


def bit_orders(replicas):
    bits = (replicas // 2).bit_length() - 1
    down = list(range(bits - 1, -1, -1))
    return (down, [0] + down[:-1] if bits else [])


def exchange(value, replicas, turn):
    orders = bit_orders(replicas)
    pairs = [(r, r ^ (2 << orders[r % 2][turn])) for r in range(replicas)]
    return lax.ppermute(value, "replica", pairs)


def swap_cores(value, replicas):
    return lax.ppermute(value, "replica", [(r, r ^ 1) for r in range(replicas)])


def offsets(replicas):
    tables = []
    for order in bit_orders(replicas):
        places = [0]
        for bit in order:
            places = places + [place ^ (1 << bit) for place in places]
        tables.append(places)
    return tables


def chip_at(replica, core, table, place):
    return (replica // 2) ^ jnp.where(core == 0, table[0][place], table[1][place])


def gather_shares(share):
    replicas = lax.axis_size("replica")
    replica = lax.axis_index("replica")
    core = replica % 2
    table = offsets(replicas)
    held = share[None]
    for turn in range(len(table[0]).bit_length() - 1):
        held = jnp.concatenate([held, exchange(held, replicas, turn)], axis=0)
    other = swap_cores(held, replicas)
    result = jnp.zeros((replicas,) + share.shape, share.dtype)
    for place in range(replicas // 2):
        mine = chip_at(replica, core, table, place) * 2 + core
        theirs = chip_at(replica, 1 - core, table, place) * 2 + 1 - core
        result = lax.dynamic_update_slice(result, held[place][None], (mine, 0, 0))
        result = lax.dynamic_update_slice(result, other[place][None], (theirs, 0, 0))
    return result


def reduce_shares(partial):
    replicas = lax.axis_size("replica")
    replica = lax.axis_index("replica")
    core = replica % 2
    table = offsets(replicas)
    halves = partial.reshape((replicas // 2, 2) + partial.shape[1:])
    sent = jnp.where(core == 0, halves[:, 1], halves[:, 0])
    kept = jnp.where(core == 0, halves[:, 0], halves[:, 1])
    total = kept.astype(jnp.float32) + swap_cores(sent, replicas).astype(jnp.float32)
    total = jnp.concatenate(
        [
            lax.dynamic_index_in_dim(total, chip_at(replica, core, table, place), 0, True)
            for place in range(replicas // 2)
        ],
        axis=0,
    )
    turns = len(table[0]).bit_length() - 1
    for turn in range(turns - 1, -1, -1):
        half = total.shape[0] // 2
        arrived = exchange(total[half:].astype(jnp.bfloat16), replicas, turn)
        total = total[:half] + arrived.astype(jnp.float32)
    return total[0]


def adam_update(weight_now, moment, second, gradient):
    moment_new = decay_first * moment + (1.0 - decay_first) * gradient
    second_new = decay_second * second + (1.0 - decay_second) * gradient * gradient
    update = (
        learn_rate
        * (moment_new / (1.0 - decay_first**step_count))
        / (jnp.sqrt(second_new / (1.0 - decay_second**step_count)) + adam_floor)
    )
    return (weight_now - update, moment_new, second_new)


def per_device(
    coords_in,
    token_rows,
    cotangent,
    subspace_basis,
    norm_gain,
    gate_weight,
    up_weight,
    down_weight,
    gate_moment,
    gate_second,
    down_moment,
    down_second,
):
    batches, rows_dev, coord_width = coords_in.shape
    model_width = subspace_basis.shape[1]
    sections = lax.axis_size("section")
    replicas = lax.axis_size("replica")
    section = lax.axis_index("section")
    share_rows, hidden_width = gate_weight.shape[1:]
    down_rows = down_weight.shape[1]
    bf16 = jnp.bfloat16

    gate_up = jnp.concatenate([gate_weight[0].astype(bf16), up_weight[0]], axis=1)
    down = down_weight[0].astype(bf16)
    packed = jnp.concatenate([gate_up, down.reshape(-1, gate_up.shape[1])], axis=0)
    gathered = gather_shares(packed)
    w_gate_up = gathered[:, :share_rows].reshape(model_width, 2 * hidden_width)
    w_down = gathered[:, share_rows:].reshape(hidden_width, coord_width)

    def put(buffer, item, slot):
        return lax.dynamic_update_index_in_dim(buffer, item, slot, 0)

    def get(buffer, slot):
        return lax.dynamic_index_in_dim(buffer, slot, 0, False)

    def room(*dims, kind=bf16):
        return jnp.zeros((batches + 1, rows_dev) + dims, kind)

    store = {
        "output": room(coord_width),
        "expanded": room(model_width, kind=jnp.float32),
        "inverse": room(1, kind=jnp.float32),
        "normed": room(model_width),
        "gate": room(hidden_width, kind=jnp.float32),
        "up": room(hidden_width, kind=jnp.float32),
        "hidden": room(hidden_width),
        "returned": room(coord_width),
        "next_grad": room(coord_width),
        "gate_grad": room(hidden_width),
    }
    blank = jnp.zeros((rows_dev, coord_width), bf16)

    def forward(tick, incoming):
        batch = tick - section
        slot = jnp.clip(batch, 0, batches)
        read = jnp.clip(batch, 0, batches - 1)
        source = jnp.where(section == 0, get(coords_in, read), incoming)
        expanded = jnp.dot(source, subspace_basis, preferred_element_type=jnp.float32) + get(
            token_rows, read
        ).astype(jnp.float32)
        inverse = lax.rsqrt(jnp.mean(expanded * expanded, axis=1, keepdims=True) + epsilon)
        normed = (expanded * inverse * norm_gain).astype(bf16)
        both = jnp.dot(normed, w_gate_up, preferred_element_type=jnp.float32)
        gate, up = both[:, :hidden_width], both[:, hidden_width:]
        hidden = (gate * jax.nn.sigmoid(gate) * up).astype(bf16)
        output = (
            source.astype(jnp.float32)
            + jnp.dot(hidden, w_down, preferred_element_type=jnp.float32)
        ).astype(bf16)
        for name, item in (
            ("output", output),
            ("expanded", expanded),
            ("inverse", inverse),
            ("normed", normed),
            ("gate", gate),
            ("up", up),
            ("hidden", hidden),
        ):
            store[name] = put(store[name], item, slot)
        return shift(output, "section", 1)

    def backward(tick, incoming):
        batch = tick - (sections - 1 - section)
        live = (batch >= 0) & (batch < batches)
        slot = jnp.clip(batch, 0, batches)
        read = jnp.clip(batch, 0, batches - 1)
        next_grad = jnp.where(section == sections - 1, get(cotangent, read), incoming)
        next_grad = jnp.where(live, next_grad, jnp.zeros_like(next_grad))
        gate, up = get(store["gate"], read), get(store["up"], read)
        expanded, inverse = get(store["expanded"], read), get(store["inverse"], read)
        hidden_grad = contract_last(next_grad, w_down)
        sigma = jax.nn.sigmoid(gate)
        gate_grad = (hidden_grad * up * (sigma * (1.0 + gate * (1.0 - sigma)))).astype(bf16)
        up_grad = (hidden_grad * (gate * sigma)).astype(bf16)
        normed_grad = contract_last(jnp.concatenate([gate_grad, up_grad], axis=1), w_gate_up)
        scaled = normed_grad * norm_gain
        centred = expanded * inverse
        expanded_grad = (
            inverse * (scaled - centred * jnp.mean(scaled * centred, axis=1, keepdims=True))
        ).astype(bf16)
        coord_grad = (
            next_grad.astype(jnp.float32) + contract_last(expanded_grad, subspace_basis)
        ).astype(bf16)
        for name, item in (
            ("returned", coord_grad),
            ("next_grad", next_grad),
            ("gate_grad", gate_grad),
        ):
            store[name] = put(store[name], item, slot)
        return shift(coord_grad, "section", -1)

    ticks = sections + batches - 1
    down_stream, up_stream = blank, blank
    for tick in range(ticks + sections - 1):
        if tick < ticks:
            down_stream = forward(tick, down_stream)
        if tick >= sections - 1:
            up_stream = backward(tick - (sections - 1), up_stream)

    def flat(name):
        return store[name][:batches].reshape(batches * rows_dev, -1)

    gate_sum = contract_first(flat("normed"), flat("gate_grad")).astype(bf16)
    down_sum = contract_first(flat("hidden"), flat("next_grad")).astype(bf16)
    down_sum = down_sum.reshape(replicas, down_rows, coord_width)
    pieces = [gate_sum.reshape(replicas, share_rows, hidden_width)]
    for start in range(0, coord_width, hidden_width):
        pieces.append(down_sum[:, :, start : start + hidden_width])
    share = reduce_shares(jnp.concatenate(pieces, axis=1))
    gate_share = share[:share_rows]
    down_share = jnp.concatenate(
        [
            share[start : start + down_rows]
            for start in range(share_rows, share.shape[0], down_rows)
        ],
        axis=1,
    )
    grad_scale = 1.0 / math.sqrt(batches * rows_dev * replicas)
    gate_new, gate_moment_new, gate_second_new = adam_update(
        gate_weight[0], gate_moment[0], gate_second[0], gate_share * grad_scale
    )
    down_new, down_moment_new, down_second_new = adam_update(
        down_weight[0], down_moment[0], down_second[0], down_share * grad_scale
    )
    return (
        store["output"][None, :batches],
        store["returned"][None, :batches],
        gate_new[None],
        gate_moment_new[None],
        gate_second_new[None],
        down_new[None],
        down_moment_new[None],
        down_second_new[None],
    )


def solution(mesh):
    rows = P(None, "replica", None)
    weight = P("section", "replica", None)
    stacked = P("section", None, "replica", None)
    return jax.shard_map(
        per_device,
        mesh=mesh,
        in_specs=(rows, rows, rows, P(), P("section", None)) + (weight,) * 7,
        out_specs=(stacked, stacked) + (weight,) * 6,
        check_vma=False,
    )
```

```python
import math

import jax
import jax.numpy as jnp
from jax import lax
from jax.experimental import pallas as pl
from jax.experimental.pallas import tpu as pltpu
from jax.sharding import PartitionSpec as P

epsilon = 1e-06
learn_rate = 0.001
decay_first = 0.9
decay_second = 0.95
step_count = 10
adam_floor = 1e-08


def contract_last(left, right):
    return lax.dot_general(
        left, right, (((1,), (1,)), ((), ())), preferred_element_type=jnp.float32
    )


def contract_first(left, right):
    return lax.dot_general(
        left, right, (((0,), (0,)), ((), ())), preferred_element_type=jnp.float32
    )


def shift(value, axis, steps):
    count = lax.axis_size(axis)
    first, last = max(0, -steps), min(count, count - steps)
    return lax.ppermute(value, axis, [(source, source + steps) for source in range(first, last)])


def bit_orders(replicas):
    bits = (replicas // 2).bit_length() - 1
    down = list(range(bits - 1, -1, -1))
    return (down, [0] + down[:-1] if bits else [])


def exchange(value, replicas, turn):
    orders = bit_orders(replicas)
    pairs = [(r, r ^ (2 << orders[r % 2][turn])) for r in range(replicas)]
    return lax.ppermute(value, "replica", pairs)


def swap_cores(value, replicas):
    return lax.ppermute(value, "replica", [(r, r ^ 1) for r in range(replicas)])


def offsets(replicas):
    tables = []
    for order in bit_orders(replicas):
        places = [0]
        for bit in order:
            places = places + [place ^ (1 << bit) for place in places]
        tables.append(places)
    return tables


def chip_at(replica, core, table, place):
    return (replica // 2) ^ jnp.where(core == 0, table[0][place], table[1][place])


def gather_shares(share):
    replicas = lax.axis_size("replica")
    replica = lax.axis_index("replica")
    core = replica % 2
    table = offsets(replicas)
    held = share[None]
    for turn in range(len(table[0]).bit_length() - 1):
        held = jnp.concatenate([held, exchange(held, replicas, turn)], axis=0)
    other = swap_cores(held, replicas)
    result = jnp.zeros((replicas,) + share.shape, share.dtype)
    for place in range(replicas // 2):
        mine = chip_at(replica, core, table, place) * 2 + core
        theirs = chip_at(replica, 1 - core, table, place) * 2 + 1 - core
        result = lax.dynamic_update_slice(result, held[place][None], (mine, 0, 0))
        result = lax.dynamic_update_slice(result, other[place][None], (theirs, 0, 0))
    return result


def reduce_shares(partial):
    replicas = lax.axis_size("replica")
    replica = lax.axis_index("replica")
    core = replica % 2
    table = offsets(replicas)
    halves = partial.reshape((replicas // 2, 2) + partial.shape[1:])
    sent = jnp.where(core == 0, halves[:, 1], halves[:, 0])
    kept = jnp.where(core == 0, halves[:, 0], halves[:, 1])
    total = kept.astype(jnp.float32) + swap_cores(sent, replicas).astype(jnp.float32)
    total = jnp.concatenate(
        [
            lax.dynamic_index_in_dim(total, chip_at(replica, core, table, place), 0, True)
            for place in range(replicas // 2)
        ],
        axis=0,
    )
    turns = len(table[0]).bit_length() - 1
    for turn in range(turns - 1, -1, -1):
        half = total.shape[0] // 2
        arrived = exchange(total[half:].astype(jnp.bfloat16), replicas, turn)
        total = total[:half] + arrived.astype(jnp.float32)
    return total[0]


def adam_update(weight_now, moment, second, gradient):
    moment_new = decay_first * moment + (1.0 - decay_first) * gradient
    second_new = decay_second * second + (1.0 - decay_second) * gradient * gradient
    update = (
        learn_rate
        * (moment_new / (1.0 - decay_first**step_count))
        / (jnp.sqrt(second_new / (1.0 - decay_second**step_count)) + adam_floor)
    )
    return (weight_now - update, moment_new, second_new)


WIDE = 512


def call(kernel, outs, *args, scratch=(), flops=0, limit=24 << 20):
    moved = sum(math.prod(a.shape) * a.dtype.itemsize for a in args)
    moved += sum(math.prod(o.shape) * o.dtype.itemsize for o in outs)
    spaces = [
        pltpu.SMEM if a.dtype == jnp.int32 else pltpu.VMEM
        for a in args
    ]
    return pl.pallas_call(
        kernel,
        out_shape=outs,
        in_specs=[pl.BlockSpec(memory_space=space) for space in spaces],
        out_specs=[pl.BlockSpec(memory_space=pltpu.VMEM)] * len(outs),
        scratch_shapes=scratch,
        compiler_params=pltpu.CompilerParams(vmem_limit_bytes=limit),
        cost_estimate=pl.CostEstimate(flops=flops, bytes_accessed=moved, transcendentals=0),
    )(*args)


def spec(shape, kind):
    return jax.ShapeDtypeStruct(tuple(shape), kind)


def blocks_of(width):
    size = min(WIDE, width)
    return [slice(start, start + size) for start in range(0, width, size)]


def dot(left, right):
    return jnp.dot(left, right, preferred_element_type=jnp.float32)


def pack_kernel(gate, up, down, packed):
    rows, width = gate.shape
    packed[:rows, :width] = gate[...].astype(jnp.bfloat16)
    packed[:rows, width:] = up[...]
    packed[rows:, :] = down[...].astype(jnp.bfloat16)


def expand(source, basis, tokens, expanded):
    width = expanded.shape[1]
    squares = 0.0
    for part in blocks_of(width):
        piece = dot(source, basis[:, part]) + tokens[:, part].astype(jnp.float32)
        expanded[:, part] = piece
        squares = squares + jnp.sum(piece * piece, axis=1, keepdims=True)
    return lax.rsqrt(squares * (1.0 / width) + epsilon)


def expand_kernel(source, basis, tokens, gain, expanded, normed, inverse):
    inv = expand(source[...], basis, tokens, expanded)
    inverse[...] = jnp.broadcast_to(inv, inverse.shape)
    for part in blocks_of(normed.shape[1]):
        normed[:, part] = (expanded[:, part] * inv * gain[:, part]).astype(jnp.bfloat16)


def act(both):
    width = both.shape[1] // 2
    gate, up = both[:, :width], both[:, width:]
    sigma = jax.nn.sigmoid(gate)
    return gate, up, sigma


def front(source, normed, w_gate_up, w_down):
    both = 0.0
    for part in blocks_of(normed.shape[1]):
        both = both + dot(normed[:, part], w_gate_up[part, :])
    gate, up, sigma = act(both)
    hidden = (gate * sigma * up).astype(jnp.bfloat16)
    output = (source.astype(jnp.float32) + dot(hidden, w_down[...])).astype(jnp.bfloat16)
    return both, hidden, output


def front_kernel(where, held, other, normed, source, w_gate_up, w_down, both, hidden, *outputs):
    places, share, _ = held.shape
    rows = w_gate_up.shape[0] // (2 * places)
    extra = share - rows
    for index in range(2 * places):
        block = held if index < places else other
        place = index % places
        target = where[index]
        w_gate_up[pl.ds(pl.multiple_of(target * rows, rows), rows), :] = block[place, :rows, :]
        w_down[pl.ds(pl.multiple_of(target * extra, extra), extra), :] = block[place, rows:, :]
    count = source.shape[0] // len(outputs)
    both[...], hidden[...], output = front(source[...], normed, w_gate_up, w_down)
    for index, out in enumerate(outputs):
        out[...] = output[index * count : (index + 1) * count]


def back(next_grad, both, expanded, inv, gain, w_gate_up, w_down, basis, scaled):
    gate, up, sigma = act(both)
    hidden_grad = contract_last(next_grad, w_down[...])
    gate_grad = (hidden_grad * up * (sigma * (1.0 + gate * (1.0 - sigma)))).astype(jnp.bfloat16)
    up_grad = (hidden_grad * (gate * sigma)).astype(jnp.bfloat16)
    grads = jnp.concatenate([gate_grad, up_grad], axis=1)
    width = expanded.shape[1]
    total = 0.0
    for part in blocks_of(width):
        piece = contract_last(grads, w_gate_up[part, :]) * gain[:, part]
        scaled[:, part] = piece
        total = total + jnp.sum(piece * expanded[:, part], axis=1, keepdims=True)
    mean = total * inv * (1.0 / width)
    coord_grad = next_grad.astype(jnp.float32)
    for part in blocks_of(width):
        piece = inv * (scaled[:, part] - expanded[:, part] * inv * mean)
        coord_grad = coord_grad + contract_last(piece.astype(jnp.bfloat16), basis[:, part])
    return gate_grad, coord_grad.astype(jnp.bfloat16)


def middle_kernel(
    source, cot, basis, tokens, gain, w_gate_up, w_down,
    output, coord_grad, normed, hidden, gate_grad, expanded, scaled,
):
    start = source[...]
    inv = expand(start, basis, tokens, expanded)
    for part in blocks_of(normed.shape[1]):
        normed[:, part] = (expanded[:, part] * inv * gain[:, part]).astype(jnp.bfloat16)
    both, hidden[...], output[...] = front(start, normed, w_gate_up, w_down)
    gate_grad[...], coord_grad[...] = back(
        cot[...], both, expanded, inv, gain, w_gate_up, w_down, basis, scaled
    )


def back_kernel(
    next_grad, both, expanded, inverse, gain, w_gate_up, w_down, basis, coord_grad, gate_grad, scaled
):
    gate_grad[...], coord_grad[...] = back(
        next_grad[...], both, expanded, inverse[:, :1], gain, w_gate_up, w_down, basis, scaled
    )


def grads_kernel(where, *refs):
    *inputs, kept, sent, normed, hidden, gate_grad, next_grad, gate_all, down_all = refs
    half = len(inputs) // 2
    places, share, width = kept.shape
    count = inputs[1].shape[0]

    def load(group):
        for batch in range(len(group) // 4):
            rows = pl.ds(batch * count, count)
            for target, value in zip((normed, hidden, gate_grad, next_grad), group[4 * batch : 4 * batch + 4]):
                target[rows, :] = value[...]

    own = where[2 * places]

    @pl.when(own == 0)
    def _():
        load(inputs[:half])

    @pl.when(own != 0)
    def _():
        load(inputs[half:])

    for part in blocks_of(normed.shape[1]):
        gate_all[part, :] = contract_first(normed[:, part], gate_grad[...])
    down_all[...] = contract_first(hidden[...], next_grad[...])
    rows = gate_all.shape[0] // (2 * places)
    extra = down_all.shape[0] // (2 * places)
    for index in range(2 * places):
        block = kept if index < places else sent
        place = index % places
        target = where[index]
        block[place, :rows, :] = gate_all[
            pl.ds(pl.multiple_of(target * rows, rows), rows), :
        ].astype(block.dtype)
        lines = down_all[pl.ds(pl.multiple_of(target * extra, extra), extra), :].astype(block.dtype)
        for turn in range(lines.shape[1] // width):
            low = rows + turn * extra
            block[place, low : low + extra, :] = lines[:, turn * width : (turn + 1) * width]


def places_of(replicas, replica):
    core = replica % 2
    table = offsets(replicas)
    result = []
    for which in (core, 1 - core):
        for place in range(replicas // 2):
            result.append(chip_at(replica, which, table, place) * 2 + which)
    return result


def two_sections(
    coords_in, token_rows, cotangent, basis, gain, gate_weight, up_weight, down_weight,
    gate_moment, gate_second, down_moment, down_second,
):
    batches, rows, coord_width = coords_in.shape
    model_width = basis.shape[1]
    replicas = lax.axis_size("replica")
    replica = lax.axis_index("replica")
    section = lax.axis_index("section")
    share_rows, width = gate_weight.shape[1:]
    down_rows = down_weight.shape[1]
    bf16, f32 = jnp.bfloat16, jnp.float32
    hidden_width = down_rows * replicas
    full = batches * rows
    where = jnp.stack([*places_of(replicas, replica), section]).astype(jnp.int32)

    (packed,) = call(
        pack_kernel, [spec((share_rows + down_rows, 2 * width), bf16)],
        gate_weight[0], up_weight[0], down_weight[0],
    )
    held = packed[None]
    turns = (replicas // 2).bit_length() - 1
    source = coords_in.reshape(full, coord_width)
    tokens = token_rows.reshape(full, model_width)
    expanded, normed, inverse = call(
        expand_kernel,
        [spec((full, model_width), f32), spec((full, model_width), bf16), spec((full, 128), f32)],
        source, basis, tokens, gain,
        flops=2 * full * coord_width * model_width,
    )
    for turn in range(turns):
        held = jnp.concatenate([held, exchange(held, replicas, turn)], axis=0)
    other = swap_cores(held, replicas)
    row_out = spec((rows, coord_width), bf16)
    w_gate_up, w_down, both, hidden, *outputs = call(
        front_kernel,
        [
            spec((model_width, 2 * width), bf16), spec((hidden_width, coord_width), bf16),
            spec((full, 2 * width), f32), spec((full, width), bf16),
        ] + [row_out] * batches,
        where, held, other, normed, source,
        flops=4 * full * width * model_width,
    )
    incoming = [shift(out, "section", 1) for out in outputs]
    made, grads, group1 = [], [], []
    for batch in range(batches):
        output, coord_grad, normed1, hidden1, gate_grad1 = call(
            middle_kernel,
            [row_out, row_out, spec((rows, model_width), bf16), spec((rows, width), bf16), spec((rows, width), bf16)],
            incoming[batch], cotangent[batch], basis, token_rows[batch], gain, w_gate_up, w_down,
            scratch=[pltpu.VMEM((rows, model_width), f32), pltpu.VMEM((rows, model_width), f32)],
            flops=8 * rows * coord_width * model_width,
        )
        made.append(output)
        grads.append(coord_grad)
        group1 += [normed1, hidden1, gate_grad1, cotangent[batch]]
    arrived = [shift(grad, "section", -1) for grad in grads]
    first_grads, group0 = [], []
    for batch in range(batches):
        part = slice(batch * rows, (batch + 1) * rows)
        coord_grad, gate_grad = call(
            back_kernel, [row_out, spec((rows, width), bf16)],
            arrived[batch], both[part], expanded[part], inverse[part], gain, w_gate_up, w_down, basis,
            scratch=[pltpu.VMEM((rows, model_width), f32)],
            flops=4 * rows * coord_width * model_width,
        )
        first_grads.append(coord_grad)
        group0 += [normed[part], hidden[part], gate_grad, arrived[batch]]
    block = spec((replicas // 2, share_rows + down_rows * (coord_width // width), width), bf16)
    kept, sent = call(
        grads_kernel, [spec(block.shape, f32), block],
        where, *group0, *group1,
        scratch=[
            pltpu.VMEM((full, model_width), bf16), pltpu.VMEM((full, width), bf16),
            pltpu.VMEM((full, width), bf16), pltpu.VMEM((full, coord_width), bf16),
            pltpu.VMEM((model_width, width), f32), pltpu.VMEM((hidden_width, coord_width), f32),
        ],
        flops=2 * full * width * (model_width + coord_width),
        limit=32 << 20,
    )
    total = kept + swap_cores(sent, replicas).astype(f32)
    for turn in range(turns - 1, -1, -1):
        half = total.shape[0] // 2
        total = total[:half] + exchange(total[half:].astype(bf16), replicas, turn).astype(f32)
    share = total[0]
    gate_share = share[:share_rows]
    down_share = jnp.concatenate(
        [share[low : low + down_rows] for low in range(share_rows, share.shape[0], down_rows)], axis=1
    )
    grad_scale = 1.0 / math.sqrt(full * replicas)
    gate_new = adam_update(gate_weight[0], gate_moment[0], gate_second[0], gate_share * grad_scale)
    down_new = adam_update(down_weight[0], down_moment[0], down_second[0], down_share * grad_scale)
    first = section == 0
    produced = jnp.where(first, jnp.stack(outputs), jnp.stack(made))
    returned = jnp.where(first, jnp.stack(first_grads), jnp.stack(grads))
    return tuple(item[None] for item in (produced, returned, *gate_new, *down_new))


def per_device(
    coords_in,
    token_rows,
    cotangent,
    subspace_basis,
    norm_gain,
    gate_weight,
    up_weight,
    down_weight,
    gate_moment,
    gate_second,
    down_moment,
    down_second,
):
    batches, rows_dev, coord_width = coords_in.shape
    model_width = subspace_basis.shape[1]
    sections = lax.axis_size("section")
    replicas = lax.axis_size("replica")
    section = lax.axis_index("section")
    share_rows, hidden_width = gate_weight.shape[1:]
    down_rows = down_weight.shape[1]
    bf16 = jnp.bfloat16

    gate_up = jnp.concatenate([gate_weight[0].astype(bf16), up_weight[0]], axis=1)
    down = down_weight[0].astype(bf16)
    packed = jnp.concatenate([gate_up, down.reshape(-1, gate_up.shape[1])], axis=0)
    gathered = gather_shares(packed)
    w_gate_up = gathered[:, :share_rows].reshape(model_width, 2 * hidden_width)
    w_down = gathered[:, share_rows:].reshape(hidden_width, coord_width)

    def put(buffer, item, slot):
        return lax.dynamic_update_index_in_dim(buffer, item, slot, 0)

    def get(buffer, slot):
        return lax.dynamic_index_in_dim(buffer, slot, 0, False)

    def room(*dims, kind=bf16):
        return jnp.zeros((batches + 1, rows_dev) + dims, kind)

    store = {
        "output": room(coord_width),
        "expanded": room(model_width, kind=jnp.float32),
        "inverse": room(1, kind=jnp.float32),
        "normed": room(model_width),
        "gate": room(hidden_width, kind=jnp.float32),
        "up": room(hidden_width, kind=jnp.float32),
        "hidden": room(hidden_width),
        "returned": room(coord_width),
        "next_grad": room(coord_width),
        "gate_grad": room(hidden_width),
    }
    blank = jnp.zeros((rows_dev, coord_width), bf16)

    def forward(tick, incoming):
        batch = tick - section
        slot = jnp.clip(batch, 0, batches)
        read = jnp.clip(batch, 0, batches - 1)
        source = jnp.where(section == 0, get(coords_in, read), incoming)
        expanded = jnp.dot(source, subspace_basis, preferred_element_type=jnp.float32) + get(
            token_rows, read
        ).astype(jnp.float32)
        inverse = lax.rsqrt(jnp.mean(expanded * expanded, axis=1, keepdims=True) + epsilon)
        normed = (expanded * inverse * norm_gain).astype(bf16)
        both = jnp.dot(normed, w_gate_up, preferred_element_type=jnp.float32)
        gate, up = both[:, :hidden_width], both[:, hidden_width:]
        hidden = (gate * jax.nn.sigmoid(gate) * up).astype(bf16)
        output = (
            source.astype(jnp.float32)
            + jnp.dot(hidden, w_down, preferred_element_type=jnp.float32)
        ).astype(bf16)
        for name, item in (
            ("output", output),
            ("expanded", expanded),
            ("inverse", inverse),
            ("normed", normed),
            ("gate", gate),
            ("up", up),
            ("hidden", hidden),
        ):
            store[name] = put(store[name], item, slot)
        return shift(output, "section", 1)

    def backward(tick, incoming):
        batch = tick - (sections - 1 - section)
        live = (batch >= 0) & (batch < batches)
        slot = jnp.clip(batch, 0, batches)
        read = jnp.clip(batch, 0, batches - 1)
        next_grad = jnp.where(section == sections - 1, get(cotangent, read), incoming)
        next_grad = jnp.where(live, next_grad, jnp.zeros_like(next_grad))
        gate, up = get(store["gate"], read), get(store["up"], read)
        expanded, inverse = get(store["expanded"], read), get(store["inverse"], read)
        hidden_grad = contract_last(next_grad, w_down)
        sigma = jax.nn.sigmoid(gate)
        gate_grad = (hidden_grad * up * (sigma * (1.0 + gate * (1.0 - sigma)))).astype(bf16)
        up_grad = (hidden_grad * (gate * sigma)).astype(bf16)
        normed_grad = contract_last(jnp.concatenate([gate_grad, up_grad], axis=1), w_gate_up)
        scaled = normed_grad * norm_gain
        centred = expanded * inverse
        expanded_grad = (
            inverse * (scaled - centred * jnp.mean(scaled * centred, axis=1, keepdims=True))
        ).astype(bf16)
        coord_grad = (
            next_grad.astype(jnp.float32) + contract_last(expanded_grad, subspace_basis)
        ).astype(bf16)
        for name, item in (
            ("returned", coord_grad),
            ("next_grad", next_grad),
            ("gate_grad", gate_grad),
        ):
            store[name] = put(store[name], item, slot)
        return shift(coord_grad, "section", -1)

    ticks = sections + batches - 1
    down_stream, up_stream = blank, blank
    for tick in range(ticks + sections - 1):
        if tick < ticks:
            down_stream = forward(tick, down_stream)
        if tick >= sections - 1:
            up_stream = backward(tick - (sections - 1), up_stream)

    def flat(name):
        return store[name][:batches].reshape(batches * rows_dev, -1)

    gate_sum = contract_first(flat("normed"), flat("gate_grad")).astype(bf16)
    down_sum = contract_first(flat("hidden"), flat("next_grad")).astype(bf16)
    down_sum = down_sum.reshape(replicas, down_rows, coord_width)
    pieces = [gate_sum.reshape(replicas, share_rows, hidden_width)]
    for start in range(0, coord_width, hidden_width):
        pieces.append(down_sum[:, :, start : start + hidden_width])
    share = reduce_shares(jnp.concatenate(pieces, axis=1))
    gate_share = share[:share_rows]
    down_share = jnp.concatenate(
        [
            share[start : start + down_rows]
            for start in range(share_rows, share.shape[0], down_rows)
        ],
        axis=1,
    )
    grad_scale = 1.0 / math.sqrt(batches * rows_dev * replicas)
    gate_new, gate_moment_new, gate_second_new = adam_update(
        gate_weight[0], gate_moment[0], gate_second[0], gate_share * grad_scale
    )
    down_new, down_moment_new, down_second_new = adam_update(
        down_weight[0], down_moment[0], down_second[0], down_share * grad_scale
    )
    return (
        store["output"][None, :batches],
        store["returned"][None, :batches],
        gate_new[None],
        gate_moment_new[None],
        gate_second_new[None],
        down_new[None],
        down_moment_new[None],
        down_second_new[None],
    )


def solution(mesh):
    rows = P(None, "replica", None)
    weight = P("section", "replica", None)
    stacked = P("section", None, "replica", None)
    return jax.shard_map(
        two_sections if mesh.shape["section"] == 2 else per_device,
        mesh=mesh,
        in_specs=(rows, rows, rows, P(), P("section", None)) + (weight,) * 7,
        out_specs=(stacked, stacked) + (weight,) * 6,
        check_vma=False,
    )
```

```python
import functools
import math

import jax
import jax.numpy as jnp
from jax import lax
from jax.experimental import pallas as pl
from jax.experimental.pallas import tpu as pltpu
from jax.sharding import PartitionSpec as P

epsilon = 1e-06
learn_rate = 0.001
decay_first = 0.9
decay_second = 0.95
step_count = 10
adam_floor = 1e-08


def contract_last(left, right):
    return lax.dot_general(
        left, right, (((1,), (1,)), ((), ())), preferred_element_type=jnp.float32
    )


def contract_first(left, right):
    return lax.dot_general(
        left, right, (((0,), (0,)), ((), ())), preferred_element_type=jnp.float32
    )


def shift(value, axis, steps):
    count = lax.axis_size(axis)
    first, last = max(0, -steps), min(count, count - steps)
    return lax.ppermute(value, axis, [(source, source + steps) for source in range(first, last)])


def bit_orders(replicas):
    bits = (replicas // 2).bit_length() - 1
    down = list(range(bits - 1, -1, -1))
    return (down, [0] + down[:-1] if bits else [])


def exchange(value, replicas, turn, flip=0):
    orders = bit_orders(replicas)[:: -1 if flip else 1]
    pairs = [(r, r ^ (2 << orders[r % 2][turn])) for r in range(replicas)]
    return lax.ppermute(value, "replica", pairs)


def swap_cores(value, replicas):
    return lax.ppermute(value, "replica", [(r, r ^ 1) for r in range(replicas)])


def offsets(replicas, flip=0):
    tables = []
    for order in bit_orders(replicas)[:: -1 if flip else 1]:
        places = [0]
        for bit in order:
            places = places + [place ^ (1 << bit) for place in places]
        tables.append(places)
    return tables


def chip_at(replica, core, table, place):
    return (replica // 2) ^ jnp.where(core == 0, table[0][place], table[1][place])


def gather_shares(share):
    replicas = lax.axis_size("replica")
    replica = lax.axis_index("replica")
    core = replica % 2
    table = offsets(replicas)
    held = share[None]
    for turn in range(len(table[0]).bit_length() - 1):
        held = jnp.concatenate([held, exchange(held, replicas, turn)], axis=0)
    other = swap_cores(held, replicas)
    result = jnp.zeros((replicas,) + share.shape, share.dtype)
    for place in range(replicas // 2):
        mine = chip_at(replica, core, table, place) * 2 + core
        theirs = chip_at(replica, 1 - core, table, place) * 2 + 1 - core
        result = lax.dynamic_update_slice(result, held[place][None], (mine, 0, 0))
        result = lax.dynamic_update_slice(result, other[place][None], (theirs, 0, 0))
    return result


def reduce_shares(partial):
    replicas = lax.axis_size("replica")
    replica = lax.axis_index("replica")
    core = replica % 2
    table = offsets(replicas)
    halves = partial.reshape((replicas // 2, 2) + partial.shape[1:])
    sent = jnp.where(core == 0, halves[:, 1], halves[:, 0])
    kept = jnp.where(core == 0, halves[:, 0], halves[:, 1])
    total = kept.astype(jnp.float32) + swap_cores(sent, replicas).astype(jnp.float32)
    total = jnp.concatenate(
        [
            lax.dynamic_index_in_dim(total, chip_at(replica, core, table, place), 0, True)
            for place in range(replicas // 2)
        ],
        axis=0,
    )
    turns = len(table[0]).bit_length() - 1
    for turn in range(turns - 1, -1, -1):
        half = total.shape[0] // 2
        arrived = exchange(total[half:].astype(jnp.bfloat16), replicas, turn)
        total = total[:half] + arrived.astype(jnp.float32)
    return total[0]


def adam_update(weight_now, moment, second, gradient):
    moment_new = decay_first * moment + (1.0 - decay_first) * gradient
    second_new = decay_second * second + (1.0 - decay_second) * gradient * gradient
    update = (
        learn_rate
        * (moment_new / (1.0 - decay_first**step_count))
        / (jnp.sqrt(second_new / (1.0 - decay_second**step_count)) + adam_floor)
    )
    return (weight_now - update, moment_new, second_new)


WIDE = 512


def call(kernel, outs, *args, scratch=(), flops=0, limit=12 << 20, after=(), far=False):
    moved = sum(math.prod(a.shape) * a.dtype.itemsize for a in args)
    moved += sum(math.prod(o.shape) * o.dtype.itemsize for o in outs)
    near = pltpu.HBM if far else pltpu.VMEM
    spaces = [near] * len(args)
    skipped = len(after)

    def body(*refs):
        kernel(*refs[skipped:])

    return pl.pallas_call(
        body,
        out_shape=outs,
        in_specs=[pl.BlockSpec(memory_space=space) for space in [pl.ANY] * skipped + spaces],
        out_specs=[pl.BlockSpec(memory_space=pltpu.VMEM)] * len(outs),
        scratch_shapes=scratch,
        compiler_params=pltpu.CompilerParams(vmem_limit_bytes=limit),
        cost_estimate=pl.CostEstimate(flops=flops, bytes_accessed=moved, transcendentals=0),
    )(*after, *args)


def spec(shape, kind):
    return jax.ShapeDtypeStruct(tuple(shape), kind)


def blocks_of(width):
    size = min(WIDE, width)
    return [slice(start, start + size) for start in range(0, width, size)]


def dot(left, right):
    return jnp.dot(left, right, preferred_element_type=jnp.float32)


def pack_kernel(gate_far, up_far, down_far, packed, gate, up, down, arrived):
    rows, width = gate.shape
    copies = [
        pltpu.make_async_copy(far, near, arrived.at[index])
        for index, (far, near) in enumerate(((gate_far, gate), (up_far, up), (down_far, down)))
    ]
    for copy in copies:
        copy.start()
    for copy in copies:
        copy.wait()
    packed[:rows, :width] = gate[...].astype(jnp.bfloat16)
    packed[:rows, width:] = up[...]
    packed[rows:, :] = down[...].astype(jnp.bfloat16)


def expand(source, basis, tokens, expanded):
    width = expanded.shape[1]
    squares = 0.0
    for part in blocks_of(width):
        piece = dot(source, basis[:, part]) + tokens[:, part].astype(jnp.float32)
        expanded[:, part] = piece
        squares = squares + jnp.sum(piece * piece, axis=1, keepdims=True)
    return lax.rsqrt(squares * (1.0 / width) + epsilon)


def expand_kernel(source, basis, tokens, gain, expanded, normed, inverse):
    inv = expand(source[...], basis, tokens, expanded)
    inverse[...] = jnp.broadcast_to(inv, inverse.shape)
    for part in blocks_of(normed.shape[1]):
        normed[:, part] = (expanded[:, part] * inv * gain[:, part]).astype(jnp.bfloat16)


def act(both):
    width = both.shape[1] // 2
    gate, up = both[:, :width], both[:, width:]
    sigma = jax.nn.sigmoid(gate)
    return gate, up, sigma


def front(source, normed, w_gate_up, w_down):
    both = 0.0
    for part in blocks_of(normed.shape[1]):
        both = both + dot(normed[:, part], w_gate_up[part, :])
    gate, up, sigma = act(both)
    hidden = (gate * sigma * up).astype(jnp.bfloat16)
    output = (source.astype(jnp.float32) + dot(hidden, w_down[...])).astype(jnp.bfloat16)
    return both, hidden, output


def front_kernel(*refs):
    *shares, normed, source, w_gate_up, w_down, both, hidden, first, second = refs
    outputs = (first, second)
    places = shares[0].shape[0]
    rows = w_gate_up.shape[0] // (2 * places)
    extra = w_down.shape[0] // (2 * places)
    streams = len(shares) // 2
    for stream in range(streams):
        held, other = shares[stream], shares[streams + stream]
        cut = cuts_of(rows + extra)[stream]
        for index, target in enumerate(places_of(places, stream)):
            block = held if index < places else other
            place = index % places
            top = min(cut.stop, rows)
            base = pl.multiple_of(target * rows + cut.start, 16)
            w_gate_up[pl.ds(base, top - cut.start), :] = block[place, : top - cut.start, :]
            if cut.stop > rows:
                base = pl.multiple_of(target * extra, extra)
                w_down[pl.ds(base, extra), :] = block[place, top - cut.start :, :]
    count = source.shape[0] // len(outputs)
    both[...], hidden[...], output = front(source[...], normed, w_gate_up, w_down)
    for index, out in enumerate(outputs):
        out[...] = output[index * count : (index + 1) * count]


def back(next_grad, both, expanded, inv, gain, w_gate_up, w_down, basis, scaled):
    gate, up, sigma = act(both)
    hidden_grad = contract_last(next_grad, w_down[...])
    gate_grad = (hidden_grad * up * (sigma * (1.0 + gate * (1.0 - sigma)))).astype(jnp.bfloat16)
    up_grad = (hidden_grad * (gate * sigma)).astype(jnp.bfloat16)
    grads = jnp.concatenate([gate_grad, up_grad], axis=1)
    width = expanded.shape[1]
    total = 0.0
    for part in blocks_of(width):
        piece = contract_last(grads, w_gate_up[part, :]) * gain[:, part]
        scaled[:, part] = piece
        total = total + jnp.sum(piece * expanded[:, part], axis=1, keepdims=True)
    mean = total * inv * (1.0 / width)
    coord_grad = next_grad.astype(jnp.float32)
    for part in blocks_of(width):
        piece = inv * (scaled[:, part] - expanded[:, part] * inv * mean)
        coord_grad = coord_grad + contract_last(piece.astype(jnp.bfloat16), basis[:, part])
    return gate_grad, coord_grad.astype(jnp.bfloat16)


def middle_kernel(
    batch, source, cotangent, basis, tokens, gain, w_gate_up, w_down,
    output, coord_grad, normed, hidden, gate_grad, expanded, scaled,
):
    start = source[...]
    cot, tokens = cotangent.at[batch], tokens.at[batch]
    inv = expand(start, basis, tokens, expanded)
    for part in blocks_of(normed.shape[1]):
        normed[:, part] = (expanded[:, part] * inv * gain[:, part]).astype(jnp.bfloat16)
    both, hidden[...], output[...] = front(start, normed, w_gate_up, w_down)
    gate_grad[...], coord_grad[...] = back(
        cot[...], both, expanded, inv, gain, w_gate_up, w_down, basis, scaled
    )


def back_kernel(
    batch, next_grad, both, expanded, inverse, gain, w_gate_up, w_down, basis, coord_grad, gate_grad, scaled
):
    rows = pl.ds(batch * next_grad.shape[0], next_grad.shape[0])
    gate_grad[...], coord_grad[...] = back(
        next_grad[...], both[rows, :], expanded.at[rows], inverse[rows, :1],
        gain, w_gate_up, w_down, basis, scaled,
    )


def grads_kernel(*refs):
    *inputs, kept_a, kept_b, sent_a, sent_b, normed, hidden, gate_grad, next_grad, gate_all, down_all = refs
    normed0, hidden0, cotangent, *inputs = inputs
    batches, count, _ = cotangent.shape
    places, _, width = kept_a.shape
    section = lax.axis_index("section")

    @pl.when(section == 0)
    def _():
        normed[...] = normed0[...]
        hidden[...] = hidden0[...]
        for batch in range(batches):
            rows = pl.ds(batch * count, count)
            next_grad[rows, :] = inputs[2 * batch][...]
            gate_grad[rows, :] = inputs[2 * batch + 1][...]

    @pl.when(section != 0)
    def _():
        for batch in range(batches):
            rows = pl.ds(batch * count, count)
            group = inputs[2 * batches + 3 * batch : 2 * batches + 3 * batch + 3]
            next_grad[rows, :] = cotangent[batch]
            for target, value in zip((normed, hidden, gate_grad), group):
                target[rows, :] = value[...]

    for part in blocks_of(normed.shape[1]):
        gate_all[part, :] = contract_first(normed[:, part], gate_grad[...])
    down_all[...] = contract_first(hidden[...], next_grad[...])
    rows = gate_all.shape[0] // (2 * places)
    extra = down_all.shape[0] // (2 * places)
    share = rows + extra * (down_all.shape[1] // width)
    cuts = cuts_of(share)
    for index, target in enumerate(places_of(places, 0)):
        blocks = (kept_a, kept_b) if index < places else (sent_a, sent_b)
        place = index % places
        lines = down_all[pl.ds(pl.multiple_of(target * extra, extra), extra), :]
        for cut, block in zip(cuts, blocks):
            top = min(cut.stop, rows)
            base = pl.multiple_of(target * rows + cut.start, 16)
            block[place, : top - cut.start, :] = gate_all[pl.ds(base, top - cut.start), :].astype(block.dtype)
            if cut.stop > rows:
                for turn in range(lines.shape[1] // width):
                    low = top - cut.start + turn * extra
                    block[place, low : low + extra, :] = lines[
                        :, turn * width : (turn + 1) * width
                    ].astype(block.dtype)


def cuts_of(rows):
    first = rows // 32 * 16
    return [slice(0, first), slice(first, rows)]


def places_of(places, flip):
    replica = lax.axis_index("replica")
    core, chip = replica & 1, replica >> 1
    table = offsets(2 * places, flip)
    result = []
    for which in (core, 1 - core):
        for low, high in zip(*table):
            result.append((chip ^ jnp.where(which == 0, low, high)) * 2 + which)
    return result


def select_kernel(*refs):
    *inputs, produced, returned = refs
    batches = produced.shape[1]
    section = lax.axis_index("section")
    for index, target in enumerate((produced, returned)):
        for batch in range(batches):
            first = inputs[2 * batches * index + batch]
            second = inputs[2 * batches * index + batches + batch]

            @pl.when(section == 0)
            def _(first=first, target=target, batch=batch):
                target[0, batch] = first[...]

            @pl.when(section != 0)
            def _(second=second, target=target, batch=batch):
                target[0, batch] = second[...]


def finish_kernel(scale, *refs):
    kept_a, kept_b, come_a, come_b, gw, gm, gs, dw, dm, ds, *outs = refs
    rows = gw.shape[1]
    extra = dw.shape[1]
    parts = [kept[0] + come[0].astype(jnp.float32) for kept, come in ((kept_a, come_a), (kept_b, come_b))]
    share = jnp.concatenate(parts, axis=0) * scale
    gate = share[:rows]
    down = jnp.concatenate(
        [share[low : low + extra] for low in range(rows, share.shape[0], extra)], axis=1
    )
    for values, grad, targets in (((gw, gm, gs), gate, outs[:3]), ((dw, dm, ds), down, outs[3:])):
        results = adam_update(*(value[0] for value in values), grad)
        for target, result in zip(targets, results):
            target[0] = result


def two_sections(
    coords_in, token_rows, cotangent, basis, gain, gate_weight, up_weight, down_weight,
    gate_moment, gate_second, down_moment, down_second,
):
    batches, rows, coord_width = coords_in.shape
    model_width = basis.shape[1]
    replicas = lax.axis_size("replica")
    share_rows, width = gate_weight.shape[1:]
    down_rows = down_weight.shape[1]
    bf16, f32 = jnp.bfloat16, jnp.float32
    hidden_width = down_rows * replicas
    full = batches * rows
    (packed,) = call(
        pack_kernel, [spec((share_rows + down_rows, 2 * width), bf16)],
        gate_weight[0], up_weight[0], down_weight[0],
        scratch=[
            pltpu.VMEM((share_rows, width), f32), pltpu.VMEM((share_rows, width), bf16),
            pltpu.VMEM((down_rows, coord_width), f32), pltpu.SemaphoreType.DMA((3,)),
        ],
        far=True,
    )
    held = [packed[None, cut] for cut in cuts_of(packed.shape[0])]
    turns = (replicas // 2).bit_length() - 1
    source = coords_in.reshape(full, coord_width)
    tokens = token_rows.reshape(full, model_width)
    expanded, normed, inverse = call(
        expand_kernel,
        [spec((full, model_width), f32), spec((full, model_width), bf16), spec((full, 128), f32)],
        source, basis, tokens, gain,
        flops=2 * full * coord_width * model_width,
    )
    for turn in range(turns):
        arrived = [exchange(part, replicas, turn, flip) for flip, part in enumerate(held)]
        held = [jnp.concatenate(pair, axis=0) for pair in zip(held, arrived)]
    other = [swap_cores(part, replicas) for part in held]
    row_out = spec((rows, coord_width), bf16)
    w_gate_up, w_down, both, hidden, *outputs = call(
        front_kernel,
        [
            spec((model_width, 2 * width), bf16), spec((hidden_width, coord_width), bf16),
            spec((full, 2 * width), f32), spec((full, width), bf16),
        ] + [row_out] * batches,
        *held, *other, normed, source,
        flops=4 * full * width * model_width,
    )
    incoming = [shift(out, "section", 1) for out in outputs]
    made, grads, group1 = [], [], []
    for batch in range(batches):
        output, coord_grad, *kept = call(
            functools.partial(middle_kernel, batch),
            [row_out, row_out, spec((rows, model_width), bf16), spec((rows, width), bf16), spec((rows, width), bf16)],
            incoming[batch], cotangent, basis, token_rows, gain, w_gate_up, w_down,
            scratch=[pltpu.VMEM((rows, model_width), f32), pltpu.VMEM((rows, model_width), f32)],
            flops=8 * rows * coord_width * model_width,
            after=grads[-1:],
        )
        made.append(output)
        grads.append(coord_grad)
        group1 += kept
    arrived = [shift(grad, "section", -1) for grad in grads]
    first_grads, group0 = [], []
    for batch in range(batches):
        coord_grad, gate_grad = call(
            functools.partial(back_kernel, batch), [row_out, spec((rows, width), bf16)],
            arrived[batch], both, expanded, inverse, gain, w_gate_up, w_down, basis,
            scratch=[pltpu.VMEM((rows, model_width), f32)],
            flops=4 * rows * coord_width * model_width,
            after=first_grads[-1:],
        )
        first_grads.append(coord_grad)
        group0 += [arrived[batch], gate_grad]
    cuts = cuts_of(share_rows + down_rows * (coord_width // width))
    shapes = [(replicas // 2, cut.stop - cut.start, width) for cut in cuts]
    blocks = call(
        grads_kernel, [spec(shape, kind) for kind in (f32, bf16) for shape in shapes],
        normed, hidden, cotangent, *group0, *group1,
        scratch=[
            pltpu.VMEM((full, model_width), bf16), pltpu.VMEM((full, width), bf16),
            pltpu.VMEM((full, width), bf16), pltpu.VMEM((full, coord_width), bf16),
            pltpu.VMEM((model_width, width), f32), pltpu.VMEM((hidden_width, coord_width), f32),
        ],
        flops=2 * full * width * (model_width + coord_width),
        limit=16 << 20,
    )
    swapped = [swap_cores(sent, replicas) for sent in blocks[2:]]
    totals = [kept + sent.astype(f32) for kept, sent in zip(blocks, swapped)]
    for turn in range(turns - 1, -1, -1):
        half = totals[0].shape[0] // 2
        come = [exchange(total[half:].astype(bf16), replicas, turn) for total in totals]
        totals = [total[:half] for total in totals]
        if turn:
            totals = [total + part.astype(f32) for total, part in zip(totals, come)]
    produced, returned = call(
        select_kernel, [spec((1,) + coords_in.shape, bf16)] * 2, *outputs, *made, *first_grads, *grads
    )
    grad_scale = 1.0 / math.sqrt(full * replicas)
    weights = (gate_weight, gate_moment, gate_second, down_weight, down_moment, down_second)
    updated = call(
        functools.partial(finish_kernel, grad_scale),
        [spec(weight.shape, f32) for weight in weights],
        *totals, *come, *weights,
    )
    return (produced, returned, *updated)


def per_device(
    coords_in,
    token_rows,
    cotangent,
    subspace_basis,
    norm_gain,
    gate_weight,
    up_weight,
    down_weight,
    gate_moment,
    gate_second,
    down_moment,
    down_second,
):
    batches, rows_dev, coord_width = coords_in.shape
    model_width = subspace_basis.shape[1]
    sections = lax.axis_size("section")
    replicas = lax.axis_size("replica")
    section = lax.axis_index("section")
    share_rows, hidden_width = gate_weight.shape[1:]
    down_rows = down_weight.shape[1]
    bf16 = jnp.bfloat16

    gate_up = jnp.concatenate([gate_weight[0].astype(bf16), up_weight[0]], axis=1)
    down = down_weight[0].astype(bf16)
    packed = jnp.concatenate([gate_up, down.reshape(-1, gate_up.shape[1])], axis=0)
    gathered = gather_shares(packed)
    w_gate_up = gathered[:, :share_rows].reshape(model_width, 2 * hidden_width)
    w_down = gathered[:, share_rows:].reshape(hidden_width, coord_width)

    def put(buffer, item, slot):
        return lax.dynamic_update_index_in_dim(buffer, item, slot, 0)

    def get(buffer, slot):
        return lax.dynamic_index_in_dim(buffer, slot, 0, False)

    def room(*dims, kind=bf16):
        return jnp.zeros((batches + 1, rows_dev) + dims, kind)

    store = {
        "output": room(coord_width),
        "expanded": room(model_width, kind=jnp.float32),
        "inverse": room(1, kind=jnp.float32),
        "normed": room(model_width),
        "gate": room(hidden_width, kind=jnp.float32),
        "up": room(hidden_width, kind=jnp.float32),
        "hidden": room(hidden_width),
        "returned": room(coord_width),
        "next_grad": room(coord_width),
        "gate_grad": room(hidden_width),
    }
    blank = jnp.zeros((rows_dev, coord_width), bf16)

    def forward(tick, incoming):
        batch = tick - section
        slot = jnp.clip(batch, 0, batches)
        read = jnp.clip(batch, 0, batches - 1)
        source = jnp.where(section == 0, get(coords_in, read), incoming)
        expanded = jnp.dot(source, subspace_basis, preferred_element_type=jnp.float32) + get(
            token_rows, read
        ).astype(jnp.float32)
        inverse = lax.rsqrt(jnp.mean(expanded * expanded, axis=1, keepdims=True) + epsilon)
        normed = (expanded * inverse * norm_gain).astype(bf16)
        both = jnp.dot(normed, w_gate_up, preferred_element_type=jnp.float32)
        gate, up = both[:, :hidden_width], both[:, hidden_width:]
        hidden = (gate * jax.nn.sigmoid(gate) * up).astype(bf16)
        output = (
            source.astype(jnp.float32)
            + jnp.dot(hidden, w_down, preferred_element_type=jnp.float32)
        ).astype(bf16)
        for name, item in (
            ("output", output),
            ("expanded", expanded),
            ("inverse", inverse),
            ("normed", normed),
            ("gate", gate),
            ("up", up),
            ("hidden", hidden),
        ):
            store[name] = put(store[name], item, slot)
        return shift(output, "section", 1)

    def backward(tick, incoming):
        batch = tick - (sections - 1 - section)
        live = (batch >= 0) & (batch < batches)
        slot = jnp.clip(batch, 0, batches)
        read = jnp.clip(batch, 0, batches - 1)
        next_grad = jnp.where(section == sections - 1, get(cotangent, read), incoming)
        next_grad = jnp.where(live, next_grad, jnp.zeros_like(next_grad))
        gate, up = get(store["gate"], read), get(store["up"], read)
        expanded, inverse = get(store["expanded"], read), get(store["inverse"], read)
        hidden_grad = contract_last(next_grad, w_down)
        sigma = jax.nn.sigmoid(gate)
        gate_grad = (hidden_grad * up * (sigma * (1.0 + gate * (1.0 - sigma)))).astype(bf16)
        up_grad = (hidden_grad * (gate * sigma)).astype(bf16)
        normed_grad = contract_last(jnp.concatenate([gate_grad, up_grad], axis=1), w_gate_up)
        scaled = normed_grad * norm_gain
        centred = expanded * inverse
        expanded_grad = (
            inverse * (scaled - centred * jnp.mean(scaled * centred, axis=1, keepdims=True))
        ).astype(bf16)
        coord_grad = (
            next_grad.astype(jnp.float32) + contract_last(expanded_grad, subspace_basis)
        ).astype(bf16)
        for name, item in (
            ("returned", coord_grad),
            ("next_grad", next_grad),
            ("gate_grad", gate_grad),
        ):
            store[name] = put(store[name], item, slot)
        return shift(coord_grad, "section", -1)

    ticks = sections + batches - 1
    down_stream, up_stream = blank, blank
    for tick in range(ticks + sections - 1):
        if tick < ticks:
            down_stream = forward(tick, down_stream)
        if tick >= sections - 1:
            up_stream = backward(tick - (sections - 1), up_stream)

    def flat(name):
        return store[name][:batches].reshape(batches * rows_dev, -1)

    gate_sum = contract_first(flat("normed"), flat("gate_grad")).astype(bf16)
    down_sum = contract_first(flat("hidden"), flat("next_grad")).astype(bf16)
    down_sum = down_sum.reshape(replicas, down_rows, coord_width)
    pieces = [gate_sum.reshape(replicas, share_rows, hidden_width)]
    for start in range(0, coord_width, hidden_width):
        pieces.append(down_sum[:, :, start : start + hidden_width])
    share = reduce_shares(jnp.concatenate(pieces, axis=1))
    gate_share = share[:share_rows]
    down_share = jnp.concatenate(
        [
            share[start : start + down_rows]
            for start in range(share_rows, share.shape[0], down_rows)
        ],
        axis=1,
    )
    grad_scale = 1.0 / math.sqrt(batches * rows_dev * replicas)
    gate_new, gate_moment_new, gate_second_new = adam_update(
        gate_weight[0], gate_moment[0], gate_second[0], gate_share * grad_scale
    )
    down_new, down_moment_new, down_second_new = adam_update(
        down_weight[0], down_moment[0], down_second[0], down_share * grad_scale
    )
    return (
        store["output"][None, :batches],
        store["returned"][None, :batches],
        gate_new[None],
        gate_moment_new[None],
        gate_second_new[None],
        down_new[None],
        down_moment_new[None],
        down_second_new[None],
    )


def solution(mesh):
    rows = P(None, "replica", None)
    weight = P("section", "replica", None)
    stacked = P("section", None, "replica", None)
    return jax.shard_map(
        two_sections if mesh.shape["section"] == 2 else per_device,
        mesh=mesh,
        in_specs=(rows, rows, rows, P(), P("section", None)) + (weight,) * 7,
        out_specs=(stacked, stacked) + (weight,) * 6,
        check_vma=False,
    )
```

```python
import functools
import math

import jax
import jax.numpy as jnp
from jax import lax
from jax.experimental import pallas as pl
from jax.experimental.pallas import tpu as pltpu
from jax.sharding import PartitionSpec as P


epsilon = 1e-06
learn_rate = 0.001
decay_first = 0.9
decay_second = 0.95
step_count = 10
adam_floor = 1e-08


def contract_last(left, right):
    return lax.dot_general(
        left, right, (((1,), (1,)), ((), ())), preferred_element_type=jnp.float32
    )


def contract_first(left, right):
    return lax.dot_general(
        left, right, (((0,), (0,)), ((), ())), preferred_element_type=jnp.float32
    )


def shift(value, axis, steps):
    count = lax.axis_size(axis)
    first, last = max(0, -steps), min(count, count - steps)
    return lax.ppermute(value, axis, [(source, source + steps) for source in range(first, last)])


def bit_orders(replicas, kinds="ab"):
    bits = (replicas // 2).bit_length() - 1
    down = list(range(bits - 1, -1, -1))
    known = {"a": down, "b": down[-1:] + down[:-1], "c": down[:1] + down[-1:] + down[1:-1], "d": down[1:-1] + down[:1] + down[-1:]}
    return [known[kind] if bits > 1 else down for kind in kinds]


def exchange(value, replicas, turn, kinds="ab"):
    orders = bit_orders(replicas, kinds)
    pairs = [(r, r ^ (2 << orders[r % 2][turn])) for r in range(replicas)]
    return lax.ppermute(value, "replica", pairs)


def swap_sections(value):
    return lax.ppermute(value, "section", [(0, 1), (1, 0)])


def swap_cores(value, replicas):
    return lax.ppermute(value, "replica", [(r, r ^ 1) for r in range(replicas)])


def offsets(replicas, kinds="ab"):
    tables = []
    for order in bit_orders(replicas, kinds):
        places = [0]
        for bit in order:
            places = places + [place ^ (1 << bit) for place in places]
        tables.append(places)
    return tables


def chip_at(replica, core, table, place):
    return (replica // 2) ^ jnp.where(core == 0, table[0][place], table[1][place])


def gather_shares(share):
    replicas = lax.axis_size("replica")
    replica = lax.axis_index("replica")
    core = replica % 2
    table = offsets(replicas)
    held = share[None]
    for turn in range(len(table[0]).bit_length() - 1):
        held = jnp.concatenate([held, exchange(held, replicas, turn)], axis=0)
    other = swap_cores(held, replicas)
    result = jnp.zeros((replicas,) + share.shape, share.dtype)
    for place in range(replicas // 2):
        mine = chip_at(replica, core, table, place) * 2 + core
        theirs = chip_at(replica, 1 - core, table, place) * 2 + 1 - core
        result = lax.dynamic_update_slice(result, held[place][None], (mine, 0, 0))
        result = lax.dynamic_update_slice(result, other[place][None], (theirs, 0, 0))
    return result


def reduce_shares(partial):
    replicas = lax.axis_size("replica")
    replica = lax.axis_index("replica")
    core = replica % 2
    table = offsets(replicas)
    halves = partial.reshape((replicas // 2, 2) + partial.shape[1:])
    sent = jnp.where(core == 0, halves[:, 1], halves[:, 0])
    kept = jnp.where(core == 0, halves[:, 0], halves[:, 1])
    total = kept.astype(jnp.float32) + swap_cores(sent, replicas).astype(jnp.float32)
    total = jnp.concatenate(
        [
            lax.dynamic_index_in_dim(total, chip_at(replica, core, table, place), 0, True)
            for place in range(replicas // 2)
        ],
        axis=0,
    )
    turns = len(table[0]).bit_length() - 1
    for turn in range(turns - 1, -1, -1):
        half = total.shape[0] // 2
        arrived = exchange(total[half:].astype(jnp.bfloat16), replicas, turn)
        total = total[:half] + arrived.astype(jnp.float32)
    return total[0]


def adam_update(weight_now, moment, second, gradient):
    moment_new = decay_first * moment + (1.0 - decay_first) * gradient
    second_new = decay_second * second + (1.0 - decay_second) * gradient * gradient
    update = (
        learn_rate
        * (moment_new / (1.0 - decay_first**step_count))
        / (jnp.sqrt(second_new / (1.0 - decay_second**step_count)) + adam_floor)
    )
    return (weight_now - update, moment_new, second_new)


WIDE = 512
GATHER = ("ac", "ba")
REDUCE = ("ab", "ab")


def call(kernel, outs, *args, scratch=(), flops=0, limit=12 << 20, after=(), aliases=None):
    moved = sum(math.prod(a.shape) * a.dtype.itemsize for a in args)
    moved += sum(math.prod(o.shape) * o.dtype.itemsize for o in outs)
    spaces = [pltpu.VMEM] * len(args)
    skipped = len(after)
    aliases = {skipped + source: target for source, target in (aliases or {}).items()}

    def body(*refs):
        kernel(*refs[skipped:])

    return pl.pallas_call(
        body,
        out_shape=outs,
        in_specs=[pl.BlockSpec(memory_space=space) for space in [pl.ANY] * skipped + spaces],
        out_specs=[pl.BlockSpec(memory_space=pltpu.VMEM)] * len(outs),
        scratch_shapes=scratch,
        input_output_aliases=aliases,
        compiler_params=pltpu.CompilerParams(vmem_limit_bytes=limit),
        cost_estimate=pl.CostEstimate(flops=flops, bytes_accessed=moved, transcendentals=0),
    )(*after, *args)


def spec(shape, kind):
    return jax.ShapeDtypeStruct(tuple(shape), kind)


def blocks_of(width):
    size = min(WIDE, width)
    return [slice(start, start + size) for start in range(0, width, size)]


def dot(left, right):
    return jnp.dot(left, right, preferred_element_type=jnp.float32)


def pack_kernel(gate, down, up, packed, up_near):
    rows, width = gate.shape
    up_near[...] = up[...]
    packed[:rows, :] = gate[...].astype(jnp.bfloat16)
    for turn, low in enumerate(range(rows, packed.shape[0], down.shape[0])):
        packed[low : low + down.shape[0], :] = down[:, turn * width : (turn + 1) * width].astype(jnp.bfloat16)


def expand(source, basis, tokens, expanded):
    width = expanded.shape[1]
    squares = 0.0
    for part in blocks_of(width):
        piece = dot(source, basis[:, part]) + tokens[:, part].astype(jnp.float32)
        expanded[:, part] = piece
        squares = squares + jnp.sum(piece * piece, axis=1, keepdims=True)
    return lax.rsqrt(squares * (1.0 / width) + epsilon)


def expand_kernel(source, basis, tokens, gain, expanded, normed, inverse):
    inv = expand(source[...], basis, tokens, expanded)
    inverse[...] = jnp.broadcast_to(inv, inverse.shape)
    for part in blocks_of(normed.shape[1]):
        normed[:, part] = (expanded[:, part] * inv * gain[:, part]).astype(jnp.bfloat16)


def act(both):
    width = both.shape[1] // 2
    gate, up = both[:, :width], both[:, width:]
    sigma = jax.nn.sigmoid(gate)
    return gate, up, sigma


def front(source, normed, w_gate_up, w_down):
    both = 0.0
    for part in blocks_of(normed.shape[1]):
        both = both + dot(normed[:, part], w_gate_up[part, :])
    gate, up, sigma = act(both)
    hidden = (gate * sigma * up).astype(jnp.bfloat16)
    output = (source.astype(jnp.float32) + dot(hidden, w_down[...])).astype(jnp.bfloat16)
    return both, hidden, output


def assemble(pieces, places, first, theirs, w_gate_up, w_down):
    rows = w_gate_up.shape[0] // (2 * places)
    extra = w_down.shape[0] // (2 * places)
    width = w_gate_up.shape[1] // 2
    up, packed = pieces
    for stream in range(2):
        targets = places_of(places, GATHER[stream])[places if theirs else 0 :]
        for place in range(up.shape[0]):
            target = targets[first + place]
            lines = pl.ds(pl.multiple_of(target * rows, rows), rows)
            if stream == 0:
                w_gate_up[lines, width:] = up[place]
                continue
            w_gate_up[lines, :width] = packed[place, :rows, :]
            lines = pl.ds(pl.multiple_of(target * extra, extra), extra)
            for turn, low in enumerate(range(rows, packed.shape[1], extra)):
                w_down[lines, turn * width : (turn + 1) * width] = packed[place, low : low + extra, :]


def assemble_kernel(*refs):
    *pieces, w_gate_up, w_down = refs
    half = pieces[0].shape[0]
    for index, (first, theirs) in enumerate(((0, False), (half, False), (0, True))):
        assemble(pieces[2 * index : 2 * index + 2], 2 * half, first, theirs, w_gate_up, w_down)


def front_kernel(up, packed, part_gate_up, part_down, normed, source, w_gate_up, w_down, both, hidden, *outputs):
    half = up.shape[0]
    assemble((up, packed), 2 * half, half, True, w_gate_up, w_down)
    count = source.shape[0] // len(outputs)
    both[...], hidden[...], output = front(source[...], normed, w_gate_up, w_down)
    for index, out in enumerate(outputs):
        out[...] = output[index * count : (index + 1) * count]


def turn_kernel(*refs):
    half = len(refs) // 2
    for source, target in zip(refs[:half], refs[half:]):
        step = min(WIDE, source.shape[0])
        for low in range(0, source.shape[0], step):
            target[:, low : low + step] = source[low : low + step, :].T


def back(next_grad, both, expanded, inv, gain, gate_up_turned, down_turned, basis_turned, scaled):
    gate, up, sigma = act(both)
    hidden_grad = dot(next_grad, down_turned[...])
    gate_grad = (hidden_grad * up * (sigma * (1.0 + gate * (1.0 - sigma)))).astype(jnp.bfloat16)
    up_grad = (hidden_grad * (gate * sigma)).astype(jnp.bfloat16)
    grads = jnp.concatenate([gate_grad, up_grad], axis=1)
    width = expanded.shape[1]
    total = 0.0
    for part in blocks_of(width):
        piece = dot(grads, gate_up_turned[:, part]) * gain[:, part]
        scaled[:, part] = piece
        total = total + jnp.sum(piece * expanded[:, part], axis=1, keepdims=True)
    mean = total * inv * (1.0 / width)
    coord_grad = next_grad.astype(jnp.float32)
    for part in blocks_of(width):
        piece = inv * (scaled[:, part] - expanded[:, part] * inv * mean)
        coord_grad = coord_grad + dot(piece.astype(jnp.bfloat16), basis_turned[part, :])
    return gate_grad, coord_grad.astype(jnp.bfloat16)


def middle_kernel(
    batch, source, cotangent, basis, tokens, gain, w_gate_up, w_down,
    gate_up_turned, down_turned, basis_turned, output, coord_grad, normed, hidden, gate_grad, expanded, scaled,
):
    start = source[...]
    cot, tokens = cotangent.at[batch], tokens.at[batch]
    inv = expand(start, basis, tokens, expanded)
    for part in blocks_of(normed.shape[1]):
        normed[:, part] = (expanded[:, part] * inv * gain[:, part]).astype(jnp.bfloat16)
    both, hidden[...], output[...] = front(start, normed, w_gate_up, w_down)
    gate_grad[...], coord_grad[...] = back(
        cot[...], both, expanded, inv, gain, gate_up_turned, down_turned, basis_turned, scaled
    )


def back_kernel(
    batch, next_grad, both, expanded, inverse, gain, gate_up_turned, down_turned, basis_turned,
    coord_grad, gate_grad, scaled,
):
    rows = pl.ds(batch * next_grad.shape[0], next_grad.shape[0])
    gate_grad[...], coord_grad[...] = back(
        next_grad[...], both[rows, :], expanded.at[rows], inverse[rows, :1],
        gain, gate_up_turned, down_turned, basis_turned, scaled,
    )


def grads_kernel(*refs):
    *inputs, kept_a, kept_b, sent_a, sent_b, hidden, gate_grad, next_grad, down_all, turned = refs
    turned0, hidden0, cotangent, *inputs = inputs
    batches, count, _ = cotangent.shape
    places, _, width = kept_a.shape
    section = lax.axis_index("section")

    @pl.when(section == 0)
    def _():
        hidden[...] = hidden0[...]
        for batch in range(batches):
            rows = pl.ds(batch * count, count)
            next_grad[rows, :] = inputs[2 * batch][...]
            gate_grad[rows, :] = inputs[2 * batch + 1][...]

    @pl.when(section != 0)
    def _():
        for batch in range(batches):
            rows = pl.ds(batch * count, count)
            group = inputs[2 * batches + 3 * batch : 2 * batches + 3 * batch + 3]
            next_grad[rows, :] = cotangent[batch]
            hidden[rows, :] = group[1][...]
            gate_grad[rows, :] = group[2][...]
            for part in blocks_of(turned.shape[0]):
                turned[part, rows] = group[0][:, part].T

    down_all[...] = contract_first(hidden[...], next_grad[...])
    rows = turned.shape[0] // (2 * places)
    extra = down_all.shape[0] // (2 * places)
    cuts = cuts_of(rows + extra * (down_all.shape[1] // width))

    def fill(source):
        for index, target in enumerate(places_of(places, REDUCE[0])):
            blocks = (kept_a, kept_b) if index < places else (sent_a, sent_b)
            place = index % places
            lines = down_all[pl.ds(pl.multiple_of(target * extra, extra), extra), :]
            gate = dot(source[pl.ds(pl.multiple_of(target * rows, rows), rows), :], gate_grad[...])
            for cut, block in zip(cuts, blocks):
                top = min(cut.stop, rows)
                block[place, : top - cut.start, :] = gate[cut.start : top, :].astype(block.dtype)
                if cut.stop > rows:
                    for turn in range(lines.shape[1] // width):
                        low = top - cut.start + turn * extra
                        block[place, low : low + extra, :] = lines[
                            :, turn * width : (turn + 1) * width
                        ].astype(block.dtype)

    @pl.when(section == 0)
    def _():
        fill(turned0)

    @pl.when(section != 0)
    def _():
        fill(turned)


def cuts_of(rows):
    first = rows // 32 * 16
    return [slice(0, first), slice(first, rows)]


def places_of(places, kinds):
    replica = lax.axis_index("replica")
    core, chip = replica & 1, replica >> 1
    table = offsets(2 * places, kinds)
    result = []
    for which in (core, 1 - core):
        for low, high in zip(*table):
            result.append((chip ^ jnp.where(which == 0, low, high)) * 2 + which)
    return result


def select_kernel(*refs):
    *inputs, produced, returned = refs
    batches = produced.shape[1]
    section = lax.axis_index("section")
    for index, target in enumerate((produced, returned)):
        for batch in range(batches):
            first = inputs[2 * batches * index + batch]
            second = inputs[2 * batches * index + batches + batch]

            @pl.when(section == 0)
            def _(first=first, target=target, batch=batch):
                target[0, batch] = first[...]

            @pl.when(section != 0)
            def _(second=second, target=target, batch=batch):
                target[0, batch] = second[...]


def finish_kernel(scale, *refs):
    kept_a, kept_b, come_a, come_b, gw, gm, gs, dw, dm, ds, *outs = refs
    rows = gw.shape[1]
    extra = dw.shape[1]
    parts = [kept[0] + come[0].astype(jnp.float32) for kept, come in ((kept_a, come_a), (kept_b, come_b))]
    share = jnp.concatenate(parts, axis=0) * scale
    gate = share[:rows]
    down = jnp.concatenate(
        [share[low : low + extra] for low in range(rows, share.shape[0], extra)], axis=1
    )
    for values, grad, targets in (((gw, gm, gs), gate, outs[:3]), ((dw, dm, ds), down, outs[3:])):
        results = adam_update(*(value[0] for value in values), grad)
        for target, result in zip(targets, results):
            target[0] = result


def two_sections(
    coords_in, token_rows, cotangent, basis, gain, gate_weight, up_weight, down_weight,
    gate_moment, gate_second, down_moment, down_second,
):
    batches, rows, coord_width = coords_in.shape
    model_width = basis.shape[1]
    replicas = lax.axis_size("replica")
    share_rows, width = gate_weight.shape[1:]
    down_rows = down_weight.shape[1]
    bf16, f32 = jnp.bfloat16, jnp.float32
    hidden_width = down_rows * replicas
    full = batches * rows
    packed, up_near = call(
        pack_kernel,
        [spec((share_rows + down_rows * (coord_width // width), width), bf16), spec(up_weight.shape, bf16)],
        gate_weight[0], down_weight[0], up_weight,
    )
    held = [up_near, packed[None]]
    turns = (replicas // 2).bit_length() - 1
    source = coords_in.reshape(full, coord_width)
    tokens = token_rows.reshape(full, model_width)
    expanded, normed, inverse = call(
        expand_kernel,
        [spec((full, model_width), f32), spec((full, model_width), bf16), spec((full, 128), f32)],
        source, basis, tokens, gain,
        flops=2 * full * coord_width * model_width,
    )
    for turn in range(turns):
        if turn == turns - 1:
            *held, normed = lax.optimization_barrier((*held, normed))
        come = []
        for part, kinds, name in zip(held, GATHER, ("up", "packed")):
            sent = up_weight if turn == 0 and name == "up" else part
            come.append(exchange(sent, replicas, turn, kinds))
        if turn < turns - 1:
            held = [jnp.concatenate(pair, axis=0) for pair in zip(held, come)]
    theirs = [swap_cores(part, replicas) for part in held]
    last = [swap_cores(part, replicas) for part in come]
    weights = [spec((model_width, 2 * width), bf16), spec((hidden_width, coord_width), bf16)]
    part_gate_up, part_down = call(assemble_kernel, weights, *held, *come, *theirs)
    row_out = spec((rows, coord_width), bf16)
    w_gate_up, w_down, both, hidden, *outputs = call(
        front_kernel,
        weights + [spec((full, 2 * width), f32), spec((full, width), bf16)] + [row_out] * batches,
        *last, part_gate_up, part_down, normed, source,
        flops=4 * full * width * model_width,
        aliases={2: 0, 3: 1},
    )
    incoming = [swap_sections(outputs[0])]
    turned = call(
        turn_kernel,
        [spec(value.shape[::-1], bf16) for value in (w_gate_up, w_down, basis, normed)],
        w_gate_up, w_down, basis, normed,
        limit=16 << 20,
    )
    later, turned = lax.optimization_barrier((outputs[1:], turned))
    incoming += [swap_sections(out) for out in later]
    *turned, normed_turned = turned
    made, grads, group1 = [], [], []
    for batch in range(batches):
        output, coord_grad, *kept = call(
            functools.partial(middle_kernel, batch),
            [row_out, row_out, spec((rows, model_width), bf16), spec((rows, width), bf16), spec((rows, width), bf16)],
            incoming[batch], cotangent, basis, token_rows, gain, w_gate_up, w_down, *turned,
            scratch=[pltpu.VMEM((rows, model_width), f32), pltpu.VMEM((rows, model_width), f32)],
            flops=8 * rows * coord_width * model_width,
            after=grads[-1:],
        )
        made.append(output)
        grads.append(coord_grad)
        group1 += kept
    arrived = [swap_sections(grad) for grad in grads]
    first_grads, group0 = [], []
    for batch in range(batches):
        coord_grad, gate_grad = call(
            functools.partial(back_kernel, batch), [row_out, spec((rows, width), bf16)],
            arrived[batch], both, expanded, inverse, gain, *turned,
            scratch=[pltpu.VMEM((rows, model_width), f32)],
            flops=4 * rows * coord_width * model_width,
            after=first_grads[-1:],
        )
        first_grads.append(coord_grad)
        group0 += [arrived[batch], gate_grad]
    cuts = cuts_of(share_rows + down_rows * (coord_width // width))
    shapes = [(replicas // 2, cut.stop - cut.start, width) for cut in cuts]
    blocks = call(
        grads_kernel, [spec(shape, kind) for kind in (f32, bf16) for shape in shapes],
        normed_turned, hidden, cotangent, *group0, *group1,
        scratch=[
            pltpu.VMEM((full, width), bf16), pltpu.VMEM((full, width), bf16),
            pltpu.VMEM((full, coord_width), bf16), pltpu.VMEM((hidden_width, coord_width), f32),
            pltpu.VMEM((model_width, full), bf16),
        ],
        flops=2 * full * width * (model_width + coord_width),
        limit=16 << 20,
    )
    swapped = [swap_cores(sent, replicas) for sent in blocks[2:]]
    totals = [kept + sent.astype(f32) for kept, sent in zip(blocks, swapped)]
    for turn in range(turns - 1, -1, -1):
        half = totals[0].shape[0] // 2
        come = [
            exchange(total[half:].astype(bf16), replicas, turn, kinds) for total, kinds in zip(totals, REDUCE)
        ]
        totals = [total[:half] for total in totals]
        if turn:
            totals = [total + part.astype(f32) for total, part in zip(totals, come)]
    produced, returned = call(
        select_kernel, [spec((1,) + coords_in.shape, bf16)] * 2, *outputs, *made, *first_grads, *grads
    )
    grad_scale = 1.0 / math.sqrt(full * replicas)
    weights = (gate_weight, gate_moment, gate_second, down_weight, down_moment, down_second)
    updated = call(
        functools.partial(finish_kernel, grad_scale),
        [spec(weight.shape, f32) for weight in weights],
        *totals, *come, *weights,
    )
    return (produced, returned, *updated)


def per_device(
    coords_in,
    token_rows,
    cotangent,
    subspace_basis,
    norm_gain,
    gate_weight,
    up_weight,
    down_weight,
    gate_moment,
    gate_second,
    down_moment,
    down_second,
):
    batches, rows_dev, coord_width = coords_in.shape
    model_width = subspace_basis.shape[1]
    sections = lax.axis_size("section")
    replicas = lax.axis_size("replica")
    section = lax.axis_index("section")
    share_rows, hidden_width = gate_weight.shape[1:]
    down_rows = down_weight.shape[1]
    bf16 = jnp.bfloat16

    gate_up = jnp.concatenate([gate_weight[0].astype(bf16), up_weight[0]], axis=1)
    down = down_weight[0].astype(bf16)
    packed = jnp.concatenate([gate_up, down.reshape(-1, gate_up.shape[1])], axis=0)
    gathered = gather_shares(packed)
    w_gate_up = gathered[:, :share_rows].reshape(model_width, 2 * hidden_width)
    w_down = gathered[:, share_rows:].reshape(hidden_width, coord_width)

    def put(buffer, item, slot):
        return lax.dynamic_update_index_in_dim(buffer, item, slot, 0)

    def get(buffer, slot):
        return lax.dynamic_index_in_dim(buffer, slot, 0, False)

    def room(*dims, kind=bf16):
        return jnp.zeros((batches + 1, rows_dev) + dims, kind)

    store = {
        "output": room(coord_width),
        "expanded": room(model_width, kind=jnp.float32),
        "inverse": room(1, kind=jnp.float32),
        "normed": room(model_width),
        "gate": room(hidden_width, kind=jnp.float32),
        "up": room(hidden_width, kind=jnp.float32),
        "hidden": room(hidden_width),
        "returned": room(coord_width),
        "next_grad": room(coord_width),
        "gate_grad": room(hidden_width),
    }
    blank = jnp.zeros((rows_dev, coord_width), bf16)

    def forward(tick, incoming):
        batch = tick - section
        slot = jnp.clip(batch, 0, batches)
        read = jnp.clip(batch, 0, batches - 1)
        source = jnp.where(section == 0, get(coords_in, read), incoming)
        expanded = jnp.dot(source, subspace_basis, preferred_element_type=jnp.float32) + get(
            token_rows, read
        ).astype(jnp.float32)
        inverse = lax.rsqrt(jnp.mean(expanded * expanded, axis=1, keepdims=True) + epsilon)
        normed = (expanded * inverse * norm_gain).astype(bf16)
        both = jnp.dot(normed, w_gate_up, preferred_element_type=jnp.float32)
        gate, up = both[:, :hidden_width], both[:, hidden_width:]
        hidden = (gate * jax.nn.sigmoid(gate) * up).astype(bf16)
        output = (
            source.astype(jnp.float32)
            + jnp.dot(hidden, w_down, preferred_element_type=jnp.float32)
        ).astype(bf16)
        for name, item in (
            ("output", output),
            ("expanded", expanded),
            ("inverse", inverse),
            ("normed", normed),
            ("gate", gate),
            ("up", up),
            ("hidden", hidden),
        ):
            store[name] = put(store[name], item, slot)
        return shift(output, "section", 1)

    def backward(tick, incoming):
        batch = tick - (sections - 1 - section)
        live = (batch >= 0) & (batch < batches)
        slot = jnp.clip(batch, 0, batches)
        read = jnp.clip(batch, 0, batches - 1)
        next_grad = jnp.where(section == sections - 1, get(cotangent, read), incoming)
        next_grad = jnp.where(live, next_grad, jnp.zeros_like(next_grad))
        gate, up = get(store["gate"], read), get(store["up"], read)
        expanded, inverse = get(store["expanded"], read), get(store["inverse"], read)
        hidden_grad = contract_last(next_grad, w_down)
        sigma = jax.nn.sigmoid(gate)
        gate_grad = (hidden_grad * up * (sigma * (1.0 + gate * (1.0 - sigma)))).astype(bf16)
        up_grad = (hidden_grad * (gate * sigma)).astype(bf16)
        normed_grad = contract_last(jnp.concatenate([gate_grad, up_grad], axis=1), w_gate_up)
        scaled = normed_grad * norm_gain
        centred = expanded * inverse
        expanded_grad = (
            inverse * (scaled - centred * jnp.mean(scaled * centred, axis=1, keepdims=True))
        ).astype(bf16)
        coord_grad = (
            next_grad.astype(jnp.float32) + contract_last(expanded_grad, subspace_basis)
        ).astype(bf16)
        for name, item in (
            ("returned", coord_grad),
            ("next_grad", next_grad),
            ("gate_grad", gate_grad),
        ):
            store[name] = put(store[name], item, slot)
        return shift(coord_grad, "section", -1)

    ticks = sections + batches - 1
    down_stream, up_stream = blank, blank
    for tick in range(ticks + sections - 1):
        if tick < ticks:
            down_stream = forward(tick, down_stream)
        if tick >= sections - 1:
            up_stream = backward(tick - (sections - 1), up_stream)

    def flat(name):
        return store[name][:batches].reshape(batches * rows_dev, -1)

    gate_sum = contract_first(flat("normed"), flat("gate_grad")).astype(bf16)
    down_sum = contract_first(flat("hidden"), flat("next_grad")).astype(bf16)
    down_sum = down_sum.reshape(replicas, down_rows, coord_width)
    pieces = [gate_sum.reshape(replicas, share_rows, hidden_width)]
    for start in range(0, coord_width, hidden_width):
        pieces.append(down_sum[:, :, start : start + hidden_width])
    share = reduce_shares(jnp.concatenate(pieces, axis=1))
    gate_share = share[:share_rows]
    down_share = jnp.concatenate(
        [
            share[start : start + down_rows]
            for start in range(share_rows, share.shape[0], down_rows)
        ],
        axis=1,
    )
    grad_scale = 1.0 / math.sqrt(batches * rows_dev * replicas)
    gate_new, gate_moment_new, gate_second_new = adam_update(
        gate_weight[0], gate_moment[0], gate_second[0], gate_share * grad_scale
    )
    down_new, down_moment_new, down_second_new = adam_update(
        down_weight[0], down_moment[0], down_second[0], down_share * grad_scale
    )
    return (
        store["output"][None, :batches],
        store["returned"][None, :batches],
        gate_new[None],
        gate_moment_new[None],
        gate_second_new[None],
        down_new[None],
        down_moment_new[None],
        down_second_new[None],
    )


def solution(mesh):
    rows = P(None, "replica", None)
    weight = P("section", "replica", None)
    stacked = P("section", None, "replica", None)
    two = mesh.shape["section"] == 2

    def body(*values):
        return (two_sections if two else per_device)(*values)

    return jax.shard_map(
        body,
        mesh=mesh,
        in_specs=(rows, rows, rows, P(), P("section", None)) + (weight,) * 7,
        out_specs=(stacked, stacked) + (weight,) * 6,
        check_vma=False,
    )
```

```python
import functools
import math

import jax
import jax.numpy as jnp
from jax import lax
from jax.experimental import pallas as pl
from jax.experimental.pallas import tpu as pltpu
from jax.sharding import PartitionSpec as P


epsilon = 1e-06
learn_rate = 0.001
decay_first = 0.9
decay_second = 0.95
step_count = 10
adam_floor = 1e-08


def contract_last(left, right):
    return lax.dot_general(
        left, right, (((1,), (1,)), ((), ())), preferred_element_type=jnp.float32
    )


def contract_first(left, right):
    return lax.dot_general(
        left, right, (((0,), (0,)), ((), ())), preferred_element_type=jnp.float32
    )


def shift(value, axis, steps):
    count = lax.axis_size(axis)
    first, last = max(0, -steps), min(count, count - steps)
    return lax.ppermute(value, axis, [(source, source + steps) for source in range(first, last)])


def bit_orders(replicas, kinds="ab"):
    bits = (replicas // 2).bit_length() - 1
    down = list(range(bits - 1, -1, -1))
    known = {"a": down, "b": down[-1:] + down[:-1], "c": down[:1] + down[-1:] + down[1:-1], "d": down[1:-1] + down[:1] + down[-1:]}
    return [known[kind] if bits > 1 else down for kind in kinds]


def exchange(value, replicas, turn, kinds="ab"):
    orders = bit_orders(replicas, kinds)
    pairs = [(r, r ^ (2 << orders[r % 2][turn])) for r in range(replicas)]
    return lax.ppermute(value, "replica", pairs)


def swap_sections(value):
    return lax.ppermute(value, "section", [(0, 1), (1, 0)])


def swap_cores(value, replicas):
    return lax.ppermute(value, "replica", [(r, r ^ 1) for r in range(replicas)])


def offsets(replicas, kinds="ab"):
    tables = []
    for order in bit_orders(replicas, kinds):
        places = [0]
        for bit in order:
            places = places + [place ^ (1 << bit) for place in places]
        tables.append(places)
    return tables


def chip_at(replica, core, table, place):
    return (replica // 2) ^ jnp.where(core == 0, table[0][place], table[1][place])


def gather_shares(share):
    replicas = lax.axis_size("replica")
    replica = lax.axis_index("replica")
    core = replica % 2
    table = offsets(replicas)
    held = share[None]
    for turn in range(len(table[0]).bit_length() - 1):
        held = jnp.concatenate([held, exchange(held, replicas, turn)], axis=0)
    other = swap_cores(held, replicas)
    result = jnp.zeros((replicas,) + share.shape, share.dtype)
    for place in range(replicas // 2):
        mine = chip_at(replica, core, table, place) * 2 + core
        theirs = chip_at(replica, 1 - core, table, place) * 2 + 1 - core
        result = lax.dynamic_update_slice(result, held[place][None], (mine, 0, 0))
        result = lax.dynamic_update_slice(result, other[place][None], (theirs, 0, 0))
    return result


def reduce_shares(partial):
    replicas = lax.axis_size("replica")
    replica = lax.axis_index("replica")
    core = replica % 2
    table = offsets(replicas)
    halves = partial.reshape((replicas // 2, 2) + partial.shape[1:])
    sent = jnp.where(core == 0, halves[:, 1], halves[:, 0])
    kept = jnp.where(core == 0, halves[:, 0], halves[:, 1])
    total = kept.astype(jnp.float32) + swap_cores(sent, replicas).astype(jnp.float32)
    total = jnp.concatenate(
        [
            lax.dynamic_index_in_dim(total, chip_at(replica, core, table, place), 0, True)
            for place in range(replicas // 2)
        ],
        axis=0,
    )
    turns = len(table[0]).bit_length() - 1
    for turn in range(turns - 1, -1, -1):
        half = total.shape[0] // 2
        arrived = exchange(total[half:].astype(jnp.bfloat16), replicas, turn)
        total = total[:half] + arrived.astype(jnp.float32)
    return total[0]


def adam_update(weight_now, moment, second, gradient):
    moment_new = decay_first * moment + (1.0 - decay_first) * gradient
    second_new = decay_second * second + (1.0 - decay_second) * gradient * gradient
    update = (
        learn_rate
        * (moment_new / (1.0 - decay_first**step_count))
        / (jnp.sqrt(second_new / (1.0 - decay_second**step_count)) + adam_floor)
    )
    return (weight_now - update, moment_new, second_new)


WIDE = 512
GATHER = ("ac", "ba")
REDUCE = ("ac", "ac")


def call(kernel, outs, *args, scratch=(), flops=0, limit=12 << 20, after=(), aliases=None):
    moved = sum(math.prod(a.shape) * a.dtype.itemsize for a in args)
    moved += sum(math.prod(o.shape) * o.dtype.itemsize for o in outs)
    spaces = [pltpu.VMEM] * len(args)
    skipped = len(after)
    aliases = {skipped + source: target for source, target in (aliases or {}).items()}

    def body(*refs):
        kernel(*refs[skipped:])

    return pl.pallas_call(
        body,
        out_shape=outs,
        in_specs=[pl.BlockSpec(memory_space=space) for space in [pl.ANY] * skipped + spaces],
        out_specs=[pl.BlockSpec(memory_space=pltpu.VMEM)] * len(outs),
        scratch_shapes=scratch,
        input_output_aliases=aliases,
        compiler_params=pltpu.CompilerParams(vmem_limit_bytes=limit),
        cost_estimate=pl.CostEstimate(flops=flops, bytes_accessed=moved, transcendentals=0),
    )(*after, *args)


def spec(shape, kind):
    return jax.ShapeDtypeStruct(tuple(shape), kind)


def blocks_of(width):
    size = min(WIDE, width)
    return [slice(start, start + size) for start in range(0, width, size)]


def dot(left, right):
    return jnp.dot(left, right, preferred_element_type=jnp.float32)


def near_kernel(value, near):
    near[...] = value[...]


def expand(source, basis, tokens, expanded):
    width = expanded.shape[1]
    squares = 0.0
    for part in blocks_of(width):
        piece = dot(source, basis[:, part]) + tokens[:, part].astype(jnp.float32)
        expanded[:, part] = piece
        squares = squares + jnp.sum(piece * piece, axis=1, keepdims=True)
    return lax.rsqrt(squares * (1.0 / width) + epsilon)


def expand_kernel(source, basis, tokens, gain, expanded, normed, inverse):
    inv = expand(source[...], basis, tokens, expanded)
    inverse[...] = jnp.broadcast_to(inv, inverse.shape)
    for part in blocks_of(normed.shape[1]):
        normed[:, part] = (expanded[:, part] * inv * gain[:, part]).astype(jnp.bfloat16)


def act(both):
    width = both.shape[1] // 2
    gate, up = both[:, :width], both[:, width:]
    sigma = jax.nn.sigmoid(gate)
    return gate, up, sigma


def front(source, normed, w_gate_up, w_down):
    both = 0.0
    for part in blocks_of(normed.shape[1]):
        both = both + dot(normed[:, part], w_gate_up[part, :])
    gate, up, sigma = act(both)
    hidden = (gate * sigma * up).astype(jnp.bfloat16)
    output = (source.astype(jnp.float32) + dot(hidden, w_down[...])).astype(jnp.bfloat16)
    return both, hidden, output


def assemble(pieces, places, first, theirs, w_gate_up, w_down):
    rows = w_gate_up.shape[0] // (2 * places)
    extra = w_down.shape[0] // (2 * places)
    width = w_gate_up.shape[1] // 2
    up, packed = pieces
    for stream in range(2):
        targets = places_of(places, GATHER[stream])[places if theirs else 0 :]
        for place in range(up.shape[0]):
            target = targets[first + place]
            lines = pl.ds(pl.multiple_of(target * rows, rows), rows)
            if stream == 0:
                w_gate_up[lines, width:] = up[place]
                continue
            w_gate_up[lines, :width] = packed[place, :rows, :]
            lines = pl.ds(pl.multiple_of(target * extra, extra), extra)
            for turn, low in enumerate(range(rows, packed.shape[1], extra)):
                w_down[lines, turn * width : (turn + 1) * width] = packed[place, low : low + extra, :]


def early_kernel(*refs):
    *pieces, w_gate_up, w_down = refs
    half = pieces[0].shape[0]
    for index, theirs in enumerate((False, True)):
        assemble(pieces[2 * index : 2 * index + 2], 2 * half, 0, theirs, w_gate_up, w_down)


def own_kernel(up, packed, part_gate_up, part_down, w_gate_up, w_down):
    half = up.shape[0]
    assemble((up, packed), 2 * half, half, False, w_gate_up, w_down)


def front_kernel(up, packed, part_gate_up, part_down, normed, source, w_gate_up, w_down, both, hidden, *outputs):
    half = up.shape[0]
    assemble((up, packed), 2 * half, half, True, w_gate_up, w_down)
    count = source.shape[0] // len(outputs)

    @pl.when(lax.axis_index("section") == 0)
    def _():
        both[...], hidden[...], output = front(source[...], normed, w_gate_up, w_down)
        for index, out in enumerate(outputs):
            out[...] = output[index * count : (index + 1) * count]


def turn_kernel(*refs):
    half = len(refs) // 2
    for source, target in zip(refs[:half], refs[half:]):
        step = min(WIDE, source.shape[0])
        for low in range(0, source.shape[0], step):
            target[:, low : low + step] = source[low : low + step, :].T


def back(next_grad, both, expanded, inv, gain, gate_up_turned, down_turned, basis_turned, scaled):
    gate, up, sigma = act(both)
    hidden_grad = dot(next_grad, down_turned[...])
    gate_grad = (hidden_grad * up * (sigma * (1.0 + gate * (1.0 - sigma)))).astype(jnp.bfloat16)
    up_grad = (hidden_grad * (gate * sigma)).astype(jnp.bfloat16)
    grads = jnp.concatenate([gate_grad, up_grad], axis=1)
    width = expanded.shape[1]
    total = 0.0
    for part in blocks_of(width):
        piece = dot(grads, gate_up_turned[:, part]) * gain[:, part]
        scaled[:, part] = piece
        total = total + jnp.sum(piece * expanded[:, part], axis=1, keepdims=True)
    mean = total * inv * (1.0 / width)
    coord_grad = next_grad.astype(jnp.float32)
    for part in blocks_of(width):
        piece = inv * (scaled[:, part] - expanded[:, part] * inv * mean)
        coord_grad = coord_grad + dot(piece.astype(jnp.bfloat16), basis_turned[part, :])
    return gate_grad, coord_grad.astype(jnp.bfloat16)


def middle_kernel(
    batch, source, cotangent, basis, tokens, gain, w_gate_up, w_down,
    gate_up_turned, down_turned, basis_turned, output, coord_grad, normed, hidden, gate_grad, expanded, scaled,
):
    cot, tokens = cotangent.at[batch], tokens.at[batch]

    @pl.when(lax.axis_index("section") != 0)
    def _():
        start = source[...]
        inv = expand(start, basis, tokens, expanded)
        for part in blocks_of(normed.shape[1]):
            normed[:, part] = (expanded[:, part] * inv * gain[:, part]).astype(jnp.bfloat16)
        both, hidden[...], output[...] = front(start, normed, w_gate_up, w_down)
        gate_grad[...], coord_grad[...] = back(
            cot[...], both, expanded, inv, gain, gate_up_turned, down_turned, basis_turned, scaled
        )


def back_kernel(
    batch, next_grad, both, expanded, inverse, gain, gate_up_turned, down_turned, basis_turned,
    coord_grad, gate_grad, scaled,
):
    rows = pl.ds(batch * next_grad.shape[0], next_grad.shape[0])

    @pl.when(lax.axis_index("section") == 0)
    def _():
        gate_grad[...], coord_grad[...] = back(
            next_grad[...], both[rows, :], expanded.at[rows], inverse[rows, :1],
            gain, gate_up_turned, down_turned, basis_turned, scaled,
        )


def grads_kernel(*refs):
    *inputs, kept_a, kept_b, sent_a, sent_b, hidden, gate_grad, next_grad, down_all, turned = refs
    turned0, hidden0, cotangent, *inputs = inputs
    batches, count, _ = cotangent.shape
    places, _, width = kept_a.shape
    section = lax.axis_index("section")

    @pl.when(section == 0)
    def _():
        hidden[...] = hidden0[...]
        for batch in range(batches):
            rows = pl.ds(batch * count, count)
            next_grad[rows, :] = inputs[2 * batch][...]
            gate_grad[rows, :] = inputs[2 * batch + 1][...]

    @pl.when(section != 0)
    def _():
        for batch in range(batches):
            rows = pl.ds(batch * count, count)
            group = inputs[2 * batches + 3 * batch : 2 * batches + 3 * batch + 3]
            next_grad[rows, :] = cotangent[batch]
            hidden[rows, :] = group[1][...]
            gate_grad[rows, :] = group[2][...]
            for part in blocks_of(turned.shape[0]):
                turned[part, rows] = group[0][:, part].T

    down_all[...] = contract_first(hidden[...], next_grad[...])
    rows = turned.shape[0] // (2 * places)
    extra = down_all.shape[0] // (2 * places)
    cuts = cuts_of(rows + extra * (down_all.shape[1] // width))

    def fill(source):
        for index, target in enumerate(places_of(places, REDUCE[0])):
            blocks = (kept_a, kept_b) if index < places else (sent_a, sent_b)
            place = index % places
            lines = down_all[pl.ds(pl.multiple_of(target * extra, extra), extra), :]
            gate = dot(source[pl.ds(pl.multiple_of(target * rows, rows), rows), :], gate_grad[...])
            for cut, block in zip(cuts, blocks):
                top = min(cut.stop, rows)
                block[place, : top - cut.start, :] = gate[cut.start : top, :].astype(block.dtype)
                if cut.stop > rows:
                    for turn in range(lines.shape[1] // width):
                        low = top - cut.start + turn * extra
                        block[place, low : low + extra, :] = lines[
                            :, turn * width : (turn + 1) * width
                        ].astype(block.dtype)

    @pl.when(section == 0)
    def _():
        fill(turned0)

    @pl.when(section != 0)
    def _():
        fill(turned)


def cuts_of(rows):
    first = rows // 32 * 16
    return [slice(0, first), slice(first, rows)]


def places_of(places, kinds):
    replica = lax.axis_index("replica")
    core, chip = replica & 1, replica >> 1
    table = offsets(2 * places, kinds)
    result = []
    for which in (core, 1 - core):
        for low, high in zip(*table):
            result.append((chip ^ jnp.where(which == 0, low, high)) * 2 + which)
    return result


def select_kernel(*refs):
    *inputs, produced, returned = refs
    batches = produced.shape[1]
    section = lax.axis_index("section")
    for index, target in enumerate((produced, returned)):
        for batch in range(batches):
            first = inputs[2 * batches * index + batch]
            second = inputs[2 * batches * index + batches + batch]

            @pl.when(section == 0)
            def _(first=first, target=target, batch=batch):
                target[0, batch] = first[...]

            @pl.when(section != 0)
            def _(second=second, target=target, batch=batch):
                target[0, batch] = second[...]


def finish_kernel(scale, *refs):
    kept_a, kept_b, come_a, come_b, gw, gm, gs, dw, dm, ds, *outs = refs
    rows = gw.shape[1]
    extra = dw.shape[1]
    parts = [kept[0] + come[0].astype(jnp.float32) for kept, come in ((kept_a, come_a), (kept_b, come_b))]
    share = jnp.concatenate(parts, axis=0) * scale
    gate = share[:rows]
    down = jnp.concatenate(
        [share[low : low + extra] for low in range(rows, share.shape[0], extra)], axis=1
    )
    for values, grad, targets in (((gw, gm, gs), gate, outs[:3]), ((dw, dm, ds), down, outs[3:])):
        results = adam_update(*(value[0] for value in values), grad)
        for target, result in zip(targets, results):
            target[0] = result


def two_sections(
    coords_in, token_rows, cotangent, basis, gain, gate_weight, up_weight, down_weight,
    gate_moment, gate_second, down_moment, down_second,
):
    batches, rows, coord_width = coords_in.shape
    model_width = basis.shape[1]
    replicas = lax.axis_size("replica")
    share_rows, width = gate_weight.shape[1:]
    down_rows = down_weight.shape[1]
    bf16, f32 = jnp.bfloat16, jnp.float32
    hidden_width = down_rows * replicas
    full = batches * rows
    lines = [down_weight[0, :, low : low + width] for low in range(0, coord_width, width)]
    packed = jnp.concatenate([part.astype(bf16) for part in (gate_weight[0], *lines)], axis=0)
    (up_near,) = call(near_kernel, [spec(up_weight.shape, bf16)], up_weight)
    held = [up_near, packed[None]]
    turns = (replicas // 2).bit_length() - 1
    source = coords_in.reshape(full, coord_width)
    tokens = token_rows.reshape(full, model_width)
    expanded, normed, inverse = call(
        expand_kernel,
        [spec((full, model_width), f32), spec((full, model_width), bf16), spec((full, 128), f32)],
        source, basis, tokens, gain,
        flops=2 * full * coord_width * model_width,
    )
    for turn in range(turns):
        come = []
        for part, kinds, name in zip(held, GATHER, ("up", "packed")):
            sent = up_weight if turn == 0 and name == "up" else part
            come.append(exchange(sent, replicas, turn, kinds))
        if turn < turns - 1:
            held = [jnp.concatenate(pair, axis=0) for pair in zip(held, come)]
    theirs = []
    for part, name in zip(held, ("up", "packed")):
        theirs.append(swap_cores(part, replicas))
    last = [swap_cores(part, replicas) for part in come]
    weights = [spec((model_width, 2 * width), bf16), spec((hidden_width, coord_width), bf16)]
    parts = call(early_kernel, weights, *held, *theirs)
    part_gate_up, part_down = call(own_kernel, weights, *come, *parts, aliases={2: 0, 3: 1})
    row_out = spec((rows, coord_width), bf16)
    w_gate_up, w_down, both, hidden, *outputs = call(
        front_kernel,
        weights + [spec((full, 2 * width), f32), spec((full, width), bf16)] + [row_out] * batches,
        *last, part_gate_up, part_down, normed, source,
        flops=4 * full * width * model_width,
        aliases={2: 0, 3: 1},
    )
    incoming = [swap_sections(outputs[0])]
    turned = call(
        turn_kernel,
        [spec(value.shape[::-1], bf16) for value in (w_gate_up, w_down, basis, normed)],
        w_gate_up, w_down, basis, normed,
        limit=16 << 20,
    )
    later, turned = lax.optimization_barrier((outputs[1:], turned))
    incoming += [swap_sections(out) for out in later]
    *turned, normed_turned = turned
    made, grads, group1 = [], [], []
    for batch in range(batches):
        output, coord_grad, *kept = call(
            functools.partial(middle_kernel, batch),
            [row_out, row_out, spec((rows, model_width), bf16), spec((rows, width), bf16), spec((rows, width), bf16)],
            incoming[batch], cotangent, basis, token_rows, gain, w_gate_up, w_down, *turned,
            scratch=[pltpu.VMEM((rows, model_width), f32), pltpu.VMEM((rows, model_width), f32)],
            flops=8 * rows * coord_width * model_width,
            after=grads[-1:],
        )
        made.append(output)
        grads.append(coord_grad)
        group1 += kept
    arrived = [swap_sections(grad) for grad in grads]
    first_grads, group0 = [], []
    for batch in range(batches):
        coord_grad, gate_grad = call(
            functools.partial(back_kernel, batch), [row_out, spec((rows, width), bf16)],
            arrived[batch], both, expanded, inverse, gain, *turned,
            scratch=[pltpu.VMEM((rows, model_width), f32)],
            flops=4 * rows * coord_width * model_width,
            after=first_grads[-1:],
        )
        first_grads.append(coord_grad)
        group0 += [arrived[batch], gate_grad]
    cuts = cuts_of(share_rows + down_rows * (coord_width // width))
    shapes = [(replicas // 2, cut.stop - cut.start, width) for cut in cuts]
    blocks = call(
        grads_kernel, [spec(shape, kind) for kind in (f32, bf16) for shape in shapes],
        normed_turned, hidden, cotangent, *group0, *group1,
        scratch=[
            pltpu.VMEM((full, width), bf16), pltpu.VMEM((full, width), bf16),
            pltpu.VMEM((full, coord_width), bf16), pltpu.VMEM((hidden_width, coord_width), f32),
            pltpu.VMEM((model_width, full), bf16),
        ],
        flops=2 * full * width * (model_width + coord_width),
        limit=16 << 20,
    )
    swapped = [swap_cores(sent, replicas) for sent in blocks[2:]]
    totals = [kept + sent.astype(f32) for kept, sent in zip(blocks, swapped)]
    for turn in range(turns - 1, -1, -1):
        half = totals[0].shape[0] // 2
        come = [
            exchange(total[half:].astype(bf16), replicas, turn, kinds) for total, kinds in zip(totals, REDUCE)
        ]
        totals = [total[:half] for total in totals]
        if turn:
            totals = [total + part.astype(f32) for total, part in zip(totals, come)]
    produced, returned = call(
        select_kernel, [spec((1,) + coords_in.shape, bf16)] * 2, *outputs, *made, *first_grads, *grads
    )
    grad_scale = 1.0 / math.sqrt(full * replicas)
    weights = (gate_weight, gate_moment, gate_second, down_weight, down_moment, down_second)
    updated = call(
        functools.partial(finish_kernel, grad_scale),
        [spec(weight.shape, f32) for weight in weights],
        *totals, *come, *weights,
    )
    return (produced, returned, *updated)


def per_device(
    coords_in,
    token_rows,
    cotangent,
    subspace_basis,
    norm_gain,
    gate_weight,
    up_weight,
    down_weight,
    gate_moment,
    gate_second,
    down_moment,
    down_second,
):
    batches, rows_dev, coord_width = coords_in.shape
    model_width = subspace_basis.shape[1]
    sections = lax.axis_size("section")
    replicas = lax.axis_size("replica")
    section = lax.axis_index("section")
    share_rows, hidden_width = gate_weight.shape[1:]
    down_rows = down_weight.shape[1]
    bf16 = jnp.bfloat16

    gate_up = jnp.concatenate([gate_weight[0].astype(bf16), up_weight[0]], axis=1)
    down = down_weight[0].astype(bf16)
    packed = jnp.concatenate([gate_up, down.reshape(-1, gate_up.shape[1])], axis=0)
    gathered = gather_shares(packed)
    w_gate_up = gathered[:, :share_rows].reshape(model_width, 2 * hidden_width)
    w_down = gathered[:, share_rows:].reshape(hidden_width, coord_width)

    def put(buffer, item, slot):
        return lax.dynamic_update_index_in_dim(buffer, item, slot, 0)

    def get(buffer, slot):
        return lax.dynamic_index_in_dim(buffer, slot, 0, False)

    def room(*dims, kind=bf16):
        return jnp.zeros((batches + 1, rows_dev) + dims, kind)

    store = {
        "output": room(coord_width),
        "expanded": room(model_width, kind=jnp.float32),
        "inverse": room(1, kind=jnp.float32),
        "normed": room(model_width),
        "gate": room(hidden_width, kind=jnp.float32),
        "up": room(hidden_width, kind=jnp.float32),
        "hidden": room(hidden_width),
        "returned": room(coord_width),
        "next_grad": room(coord_width),
        "gate_grad": room(hidden_width),
    }
    blank = jnp.zeros((rows_dev, coord_width), bf16)

    def forward(tick, incoming):
        batch = tick - section
        slot = jnp.clip(batch, 0, batches)
        read = jnp.clip(batch, 0, batches - 1)
        source = jnp.where(section == 0, get(coords_in, read), incoming)
        expanded = jnp.dot(source, subspace_basis, preferred_element_type=jnp.float32) + get(
            token_rows, read
        ).astype(jnp.float32)
        inverse = lax.rsqrt(jnp.mean(expanded * expanded, axis=1, keepdims=True) + epsilon)
        normed = (expanded * inverse * norm_gain).astype(bf16)
        both = jnp.dot(normed, w_gate_up, preferred_element_type=jnp.float32)
        gate, up = both[:, :hidden_width], both[:, hidden_width:]
        hidden = (gate * jax.nn.sigmoid(gate) * up).astype(bf16)
        output = (
            source.astype(jnp.float32)
            + jnp.dot(hidden, w_down, preferred_element_type=jnp.float32)
        ).astype(bf16)
        for name, item in (
            ("output", output),
            ("expanded", expanded),
            ("inverse", inverse),
            ("normed", normed),
            ("gate", gate),
            ("up", up),
            ("hidden", hidden),
        ):
            store[name] = put(store[name], item, slot)
        return shift(output, "section", 1)

    def backward(tick, incoming):
        batch = tick - (sections - 1 - section)
        live = (batch >= 0) & (batch < batches)
        slot = jnp.clip(batch, 0, batches)
        read = jnp.clip(batch, 0, batches - 1)
        next_grad = jnp.where(section == sections - 1, get(cotangent, read), incoming)
        next_grad = jnp.where(live, next_grad, jnp.zeros_like(next_grad))
        gate, up = get(store["gate"], read), get(store["up"], read)
        expanded, inverse = get(store["expanded"], read), get(store["inverse"], read)
        hidden_grad = contract_last(next_grad, w_down)
        sigma = jax.nn.sigmoid(gate)
        gate_grad = (hidden_grad * up * (sigma * (1.0 + gate * (1.0 - sigma)))).astype(bf16)
        up_grad = (hidden_grad * (gate * sigma)).astype(bf16)
        normed_grad = contract_last(jnp.concatenate([gate_grad, up_grad], axis=1), w_gate_up)
        scaled = normed_grad * norm_gain
        centred = expanded * inverse
        expanded_grad = (
            inverse * (scaled - centred * jnp.mean(scaled * centred, axis=1, keepdims=True))
        ).astype(bf16)
        coord_grad = (
            next_grad.astype(jnp.float32) + contract_last(expanded_grad, subspace_basis)
        ).astype(bf16)
        for name, item in (
            ("returned", coord_grad),
            ("next_grad", next_grad),
            ("gate_grad", gate_grad),
        ):
            store[name] = put(store[name], item, slot)
        return shift(coord_grad, "section", -1)

    ticks = sections + batches - 1
    down_stream, up_stream = blank, blank
    for tick in range(ticks + sections - 1):
        if tick < ticks:
            down_stream = forward(tick, down_stream)
        if tick >= sections - 1:
            up_stream = backward(tick - (sections - 1), up_stream)

    def flat(name):
        return store[name][:batches].reshape(batches * rows_dev, -1)

    gate_sum = contract_first(flat("normed"), flat("gate_grad")).astype(bf16)
    down_sum = contract_first(flat("hidden"), flat("next_grad")).astype(bf16)
    down_sum = down_sum.reshape(replicas, down_rows, coord_width)
    pieces = [gate_sum.reshape(replicas, share_rows, hidden_width)]
    for start in range(0, coord_width, hidden_width):
        pieces.append(down_sum[:, :, start : start + hidden_width])
    share = reduce_shares(jnp.concatenate(pieces, axis=1))
    gate_share = share[:share_rows]
    down_share = jnp.concatenate(
        [
            share[start : start + down_rows]
            for start in range(share_rows, share.shape[0], down_rows)
        ],
        axis=1,
    )
    grad_scale = 1.0 / math.sqrt(batches * rows_dev * replicas)
    gate_new, gate_moment_new, gate_second_new = adam_update(
        gate_weight[0], gate_moment[0], gate_second[0], gate_share * grad_scale
    )
    down_new, down_moment_new, down_second_new = adam_update(
        down_weight[0], down_moment[0], down_second[0], down_share * grad_scale
    )
    return (
        store["output"][None, :batches],
        store["returned"][None, :batches],
        gate_new[None],
        gate_moment_new[None],
        gate_second_new[None],
        down_new[None],
        down_moment_new[None],
        down_second_new[None],
    )


def solution(mesh):
    rows = P(None, "replica", None)
    weight = P("section", "replica", None)
    stacked = P("section", None, "replica", None)
    two = mesh.shape["section"] == 2

    def body(*values):
        return (two_sections if two else per_device)(*values)

    return jax.shard_map(
        body,
        mesh=mesh,
        in_specs=(rows, rows, rows, P(), P("section", None)) + (weight,) * 7,
        out_specs=(stacked, stacked) + (weight,) * 6,
        check_vma=False,
    )
```

```python
import functools
import math

import jax
import jax.numpy as jnp
from jax import lax
from jax.experimental import pallas as pl
from jax.experimental.pallas import tpu as pltpu
from jax.sharding import PartitionSpec as P


epsilon = 1e-06
learn_rate = 0.001
decay_first = 0.9
decay_second = 0.95
step_count = 10
adam_floor = 1e-08


def contract_last(left, right):
    return lax.dot_general(
        left, right, (((1,), (1,)), ((), ())), preferred_element_type=jnp.float32
    )


def contract_first(left, right):
    return lax.dot_general(
        left, right, (((0,), (0,)), ((), ())), preferred_element_type=jnp.float32
    )


def shift(value, axis, steps):
    count = lax.axis_size(axis)
    first, last = max(0, -steps), min(count, count - steps)
    return lax.ppermute(value, axis, [(source, source + steps) for source in range(first, last)])


def bit_orders(replicas, kinds="ab"):
    bits = (replicas // 2).bit_length() - 1
    down = list(range(bits - 1, -1, -1))
    known = {"a": down, "b": down[-1:] + down[:-1], "c": down[:1] + down[-1:] + down[1:-1], "d": down[1:-1] + down[:1] + down[-1:]}
    return [known[kind] if bits > 1 else down for kind in kinds]


def exchange(value, replicas, turn, kinds="ab"):
    orders = bit_orders(replicas, kinds)
    pairs = [(r, r ^ (2 << orders[r % 2][turn])) for r in range(replicas)]
    return lax.ppermute(value, "replica", pairs)


def swap_sections(value):
    return lax.ppermute(value, "section", [(0, 1), (1, 0)])


def swap_cores(value, replicas):
    return lax.ppermute(value, "replica", [(r, r ^ 1) for r in range(replicas)])


def offsets(replicas, kinds="ab"):
    tables = []
    for order in bit_orders(replicas, kinds):
        places = [0]
        for bit in order:
            places = places + [place ^ (1 << bit) for place in places]
        tables.append(places)
    return tables


def chip_at(replica, core, table, place):
    return (replica // 2) ^ jnp.where(core == 0, table[0][place], table[1][place])


def gather_shares(share):
    replicas = lax.axis_size("replica")
    replica = lax.axis_index("replica")
    core = replica % 2
    table = offsets(replicas)
    held = share[None]
    for turn in range(len(table[0]).bit_length() - 1):
        held = jnp.concatenate([held, exchange(held, replicas, turn)], axis=0)
    other = swap_cores(held, replicas)
    result = jnp.zeros((replicas,) + share.shape, share.dtype)
    for place in range(replicas // 2):
        mine = chip_at(replica, core, table, place) * 2 + core
        theirs = chip_at(replica, 1 - core, table, place) * 2 + 1 - core
        result = lax.dynamic_update_slice(result, held[place][None], (mine, 0, 0))
        result = lax.dynamic_update_slice(result, other[place][None], (theirs, 0, 0))
    return result


def reduce_shares(partial):
    replicas = lax.axis_size("replica")
    replica = lax.axis_index("replica")
    core = replica % 2
    table = offsets(replicas)
    halves = partial.reshape((replicas // 2, 2) + partial.shape[1:])
    sent = jnp.where(core == 0, halves[:, 1], halves[:, 0])
    kept = jnp.where(core == 0, halves[:, 0], halves[:, 1])
    total = kept.astype(jnp.float32) + swap_cores(sent, replicas).astype(jnp.float32)
    total = jnp.concatenate(
        [
            lax.dynamic_index_in_dim(total, chip_at(replica, core, table, place), 0, True)
            for place in range(replicas // 2)
        ],
        axis=0,
    )
    turns = len(table[0]).bit_length() - 1
    for turn in range(turns - 1, -1, -1):
        half = total.shape[0] // 2
        arrived = exchange(total[half:].astype(jnp.bfloat16), replicas, turn)
        total = total[:half] + arrived.astype(jnp.float32)
    return total[0]


def adam_update(weight_now, moment, second, gradient):
    moment_new = decay_first * moment + (1.0 - decay_first) * gradient
    second_new = decay_second * second + (1.0 - decay_second) * gradient * gradient
    update = (
        learn_rate
        * (moment_new / (1.0 - decay_first**step_count))
        / (jnp.sqrt(second_new / (1.0 - decay_second**step_count)) + adam_floor)
    )
    return (weight_now - update, moment_new, second_new)


WIDE = 512
GATHER = ("ac", "ba")
REDUCE = ("ac", "ac")


def call(kernel, outs, *args, scratch=(), flops=0, limit=12 << 20, after=(), aliases=None):
    moved = sum(math.prod(a.shape) * a.dtype.itemsize for a in args)
    moved += sum(math.prod(o.shape) * o.dtype.itemsize for o in outs)
    spaces = [pltpu.VMEM] * len(args)
    skipped = len(after)
    aliases = {skipped + source: target for source, target in (aliases or {}).items()}

    def body(*refs):
        kernel(*refs[skipped:])

    return pl.pallas_call(
        body,
        out_shape=outs,
        in_specs=[pl.BlockSpec(memory_space=space) for space in [pl.ANY] * skipped + spaces],
        out_specs=[pl.BlockSpec(memory_space=pltpu.VMEM)] * len(outs),
        scratch_shapes=scratch,
        input_output_aliases=aliases,
        compiler_params=pltpu.CompilerParams(vmem_limit_bytes=limit),
        cost_estimate=pl.CostEstimate(flops=flops, bytes_accessed=moved, transcendentals=0),
    )(*after, *args)


def spec(shape, kind):
    return jax.ShapeDtypeStruct(tuple(shape), kind)


def blocks_of(width):
    size = min(WIDE, width)
    return [slice(start, start + size) for start in range(0, width, size)]


def dot(left, right):
    return jnp.dot(left, right, preferred_element_type=jnp.float32)


def near_kernel(value, near):
    near[...] = value[...]


def expand(source, basis, tokens, expanded):
    width = expanded.shape[1]
    squares = 0.0
    for part in blocks_of(width):
        piece = dot(source, basis[:, part]) + tokens[:, part].astype(jnp.float32)
        expanded[:, part] = piece
        squares = squares + jnp.sum(piece * piece, axis=1, keepdims=True)
    return lax.rsqrt(squares * (1.0 / width) + epsilon)


def expand_kernel(source, basis, tokens, gain, expanded, normed, inverse):
    inv = expand(source[...], basis, tokens, expanded)
    inverse[...] = jnp.broadcast_to(inv, inverse.shape)
    for part in blocks_of(normed.shape[1]):
        normed[:, part] = (expanded[:, part] * inv * gain[:, part]).astype(jnp.bfloat16)


def act(both):
    width = both.shape[1] // 2
    gate, up = both[:, :width], both[:, width:]
    sigma = jax.nn.sigmoid(gate)
    return gate, up, sigma


def front(source, normed, w_gate_up, w_down):
    both = 0.0
    for part in blocks_of(normed.shape[1]):
        both = both + dot(normed[:, part], w_gate_up[part, :])
    gate, up, sigma = act(both)
    hidden = (gate * sigma * up).astype(jnp.bfloat16)
    output = (source.astype(jnp.float32) + dot(hidden, w_down[...])).astype(jnp.bfloat16)
    return both, hidden, output


def assemble(pieces, places, first, theirs, w_gate_up, w_down):
    rows = w_gate_up.shape[0] // (2 * places)
    extra = w_down.shape[0] // (2 * places)
    width = w_gate_up.shape[1] // 2
    up, packed = pieces
    for stream in range(2):
        targets = places_of(places, GATHER[stream])[places if theirs else 0 :]
        for place in range(up.shape[0]):
            target = targets[first + place]
            lines = pl.ds(pl.multiple_of(target * rows, rows), rows)
            if stream == 0:
                w_gate_up[lines, width:] = up[place]
                continue
            w_gate_up[lines, :width] = packed[place, :rows, :]
            lines = pl.ds(pl.multiple_of(target * extra, extra), extra)
            for turn, low in enumerate(range(rows, packed.shape[1], extra)):
                w_down[lines, turn * width : (turn + 1) * width] = packed[place, low : low + extra, :]


def early_kernel(*refs):
    *pieces, w_gate_up, w_down = refs
    half = pieces[0].shape[0]
    for index, theirs in enumerate((False, True)):
        assemble(pieces[2 * index : 2 * index + 2], 2 * half, 0, theirs, w_gate_up, w_down)


def own_kernel(up, packed, part_gate_up, part_down, w_gate_up, w_down):
    half = up.shape[0]
    assemble((up, packed), 2 * half, half, False, w_gate_up, w_down)


def front_kernel(up, packed, part_gate_up, part_down, normed, source, w_gate_up, w_down, both, hidden, *outputs):
    half = up.shape[0]
    assemble((up, packed), 2 * half, half, True, w_gate_up, w_down)
    count = source.shape[0] // len(outputs)

    @pl.when(lax.axis_index("section") == 0)
    def _():
        both[...], hidden[...], output = front(source[...], normed, w_gate_up, w_down)
        for index, out in enumerate(outputs):
            out[...] = output[index * count : (index + 1) * count]


def turn_kernel(*refs):
    half = len(refs) // 2
    for source, target in zip(refs[:half], refs[half:]):
        step = min(WIDE, source.shape[0])
        for low in range(0, source.shape[0], step):
            target[:, low : low + step] = source[low : low + step, :].T


def inner(next_grad, both, down_turned):
    gate, up, sigma = act(both)
    hidden_grad = dot(next_grad, down_turned[...])
    gate_grad = (hidden_grad * up * (sigma * (1.0 + gate * (1.0 - sigma)))).astype(jnp.bfloat16)
    up_grad = (hidden_grad * (gate * sigma)).astype(jnp.bfloat16)
    return gate_grad, up_grad


def back(next_grad, both, expanded, inv, gain, gate_up_turned, down_turned, basis_turned, scaled):
    gate_grad, up_grad = inner(next_grad, both, down_turned)
    grads = jnp.concatenate([gate_grad, up_grad], axis=1)
    width = expanded.shape[1]
    total = 0.0
    for part in blocks_of(width):
        piece = dot(grads, gate_up_turned[:, part]) * gain[:, part]
        scaled[:, part] = piece
        total = total + jnp.sum(piece * expanded[:, part], axis=1, keepdims=True)
    mean = total * inv * (1.0 / width)
    coord_grad = next_grad.astype(jnp.float32)
    for part in blocks_of(width):
        piece = inv * (scaled[:, part] - expanded[:, part] * inv * mean)
        coord_grad = coord_grad + dot(piece.astype(jnp.bfloat16), basis_turned[part, :])
    return gate_grad, coord_grad.astype(jnp.bfloat16)


def middle_kernel(
    batch, source, cotangent, basis, tokens, gain, w_gate_up, w_down,
    gate_up_turned, down_turned, basis_turned, output, coord_grad, normed, hidden, gate_grad, expanded, scaled,
):
    cot, tokens = cotangent.at[batch], tokens.at[batch]

    @pl.when(lax.axis_index("section") != 0)
    def _():
        start = source[...]
        inv = expand(start, basis, tokens, expanded)
        for part in blocks_of(normed.shape[1]):
            normed[:, part] = (expanded[:, part] * inv * gain[:, part]).astype(jnp.bfloat16)
        both, hidden[...], output[...] = front(start, normed, w_gate_up, w_down)
        gate_grad[...], coord_grad[...] = back(
            cot[...], both, expanded, inv, gain, gate_up_turned, down_turned, basis_turned, scaled
        )


def inner_kernel(batch, next_grad, both, down_turned, gate_grad):
    rows = pl.ds(batch * next_grad.shape[0], next_grad.shape[0])

    @pl.when(lax.axis_index("section") == 0)
    def _():
        gate_grad[...] = inner(next_grad[...], both[rows, :], down_turned)[0]


def back_kernel(*refs):
    both, expanded, inverse, gain, gate_up_turned, down_turned, basis_turned, *refs = refs
    *values, next_grad, scaled = refs
    half = len(values) // 2

    @pl.when(lax.axis_index("section") == 0)
    def _():
        count = values[0].shape[0]
        for batch in range(half):
            next_grad[pl.ds(batch * count, count), :] = values[batch][...]
        coord_grad = back(
            next_grad[...], both[...], expanded, inverse[:, :1],
            gain, gate_up_turned, down_turned, basis_turned, scaled,
        )[1]
        for batch in range(half):
            values[half + batch][...] = coord_grad[batch * count : (batch + 1) * count]


def grads_kernel(*refs):
    *inputs, kept_a, kept_b, sent_a, sent_b, hidden, gate_grad, next_grad, down_all, turned = refs
    turned0, hidden0, cotangent, *inputs = inputs
    batches, count, _ = cotangent.shape
    places, _, width = kept_a.shape
    section = lax.axis_index("section")

    @pl.when(section == 0)
    def _():
        hidden[...] = hidden0[...]
        for batch in range(batches):
            rows = pl.ds(batch * count, count)
            next_grad[rows, :] = inputs[2 * batch][...]
            gate_grad[rows, :] = inputs[2 * batch + 1][...]

    @pl.when(section != 0)
    def _():
        for batch in range(batches):
            rows = pl.ds(batch * count, count)
            group = inputs[2 * batches + 3 * batch : 2 * batches + 3 * batch + 3]
            next_grad[rows, :] = cotangent[batch]
            hidden[rows, :] = group[1][...]
            gate_grad[rows, :] = group[2][...]
            for part in blocks_of(turned.shape[0]):
                turned[part, rows] = group[0][:, part].T

    down_all[...] = contract_first(hidden[...], next_grad[...])
    rows = turned.shape[0] // (2 * places)
    extra = down_all.shape[0] // (2 * places)
    cuts = cuts_of(rows + extra * (down_all.shape[1] // width))

    def fill(source):
        for index, target in enumerate(places_of(places, REDUCE[0])):
            blocks = (kept_a, kept_b) if index < places else (sent_a, sent_b)
            place = index % places
            lines = down_all[pl.ds(pl.multiple_of(target * extra, extra), extra), :]
            gate = dot(source[pl.ds(pl.multiple_of(target * rows, rows), rows), :], gate_grad[...])
            for cut, block in zip(cuts, blocks):
                top = min(cut.stop, rows)
                block[place, : top - cut.start, :] = gate[cut.start : top, :].astype(block.dtype)
                if cut.stop > rows:
                    for turn in range(lines.shape[1] // width):
                        low = top - cut.start + turn * extra
                        block[place, low : low + extra, :] = lines[
                            :, turn * width : (turn + 1) * width
                        ].astype(block.dtype)

    @pl.when(section == 0)
    def _():
        fill(turned0)

    @pl.when(section != 0)
    def _():
        fill(turned)


def cuts_of(rows):
    first = rows // 32 * 16
    return [slice(0, first), slice(first, rows)]


def places_of(places, kinds):
    replica = lax.axis_index("replica")
    core, chip = replica & 1, replica >> 1
    table = offsets(2 * places, kinds)
    result = []
    for which in (core, 1 - core):
        for low, high in zip(*table):
            result.append((chip ^ jnp.where(which == 0, low, high)) * 2 + which)
    return result


def select_kernel(*refs):
    *inputs, produced, returned = refs
    batches = produced.shape[1]
    section = lax.axis_index("section")
    for index, target in enumerate((produced, returned)):
        for batch in range(batches):
            first = inputs[2 * batches * index + batch]
            second = inputs[2 * batches * index + batches + batch]

            @pl.when(section == 0)
            def _(first=first, target=target, batch=batch):
                target[0, batch] = first[...]

            @pl.when(section != 0)
            def _(second=second, target=target, batch=batch):
                target[0, batch] = second[...]


def finish_kernel(scale, *refs):
    kept_a, kept_b, come_a, come_b, gw, gm, gs, dw, dm, ds, *outs = refs
    rows = gw.shape[1]
    extra = dw.shape[1]
    parts = [kept[0] + come[0].astype(jnp.float32) for kept, come in ((kept_a, come_a), (kept_b, come_b))]
    share = jnp.concatenate(parts, axis=0) * scale
    gate = share[:rows]
    down = jnp.concatenate(
        [share[low : low + extra] for low in range(rows, share.shape[0], extra)], axis=1
    )
    for values, grad, targets in (((gw, gm, gs), gate, outs[:3]), ((dw, dm, ds), down, outs[3:])):
        results = adam_update(*(value[0] for value in values), grad)
        for target, result in zip(targets, results):
            target[0] = result


def two_sections(
    coords_in, token_rows, cotangent, basis, gain, gate_weight, up_weight, down_weight,
    gate_moment, gate_second, down_moment, down_second,
):
    batches, rows, coord_width = coords_in.shape
    model_width = basis.shape[1]
    replicas = lax.axis_size("replica")
    share_rows, width = gate_weight.shape[1:]
    down_rows = down_weight.shape[1]
    bf16, f32 = jnp.bfloat16, jnp.float32
    hidden_width = down_rows * replicas
    full = batches * rows
    lines = [down_weight[0, :, low : low + width] for low in range(0, coord_width, width)]
    packed = jnp.concatenate([part.astype(bf16) for part in (gate_weight[0], *lines)], axis=0)
    (up_near,) = call(near_kernel, [spec(up_weight.shape, bf16)], up_weight)
    held = [up_near, packed[None]]
    turns = (replicas // 2).bit_length() - 1
    source = coords_in.reshape(full, coord_width)
    tokens = token_rows.reshape(full, model_width)
    expanded, normed, inverse = call(
        expand_kernel,
        [spec((full, model_width), f32), spec((full, model_width), bf16), spec((full, 128), f32)],
        source, basis, tokens, gain,
        flops=2 * full * coord_width * model_width,
    )
    for turn in range(turns):
        come = []
        for part, kinds, name in zip(held, GATHER, ("up", "packed")):
            sent = up_weight if turn == 0 and name == "up" else part
            come.append(exchange(sent, replicas, turn, kinds))
        if turn < turns - 1:
            held = [jnp.concatenate(pair, axis=0) for pair in zip(held, come)]
    theirs = []
    for part, name in zip(held, ("up", "packed")):
        theirs.append(swap_cores(part, replicas))
    last = [swap_cores(part, replicas) for part in come]
    weights = [spec((model_width, 2 * width), bf16), spec((hidden_width, coord_width), bf16)]
    parts = call(early_kernel, weights, *held, *theirs)
    part_gate_up, part_down = call(own_kernel, weights, *come, *parts, aliases={2: 0, 3: 1})
    row_out = spec((rows, coord_width), bf16)
    w_gate_up, w_down, both, hidden, *outputs = call(
        front_kernel,
        weights + [spec((full, 2 * width), f32), spec((full, width), bf16)] + [row_out] * batches,
        *last, part_gate_up, part_down, normed, source,
        flops=4 * full * width * model_width,
        aliases={2: 0, 3: 1},
    )
    incoming = [swap_sections(outputs[0])]
    turned = call(
        turn_kernel,
        [spec(value.shape[::-1], bf16) for value in (w_gate_up, w_down, basis, normed)],
        w_gate_up, w_down, basis, normed,
        limit=16 << 20,
    )
    later, turned = lax.optimization_barrier((outputs[1:], turned))
    incoming += [swap_sections(out) for out in later]
    *turned, normed_turned = turned
    made, grads, group1 = [], [], []
    for batch in range(batches):
        output, coord_grad, *kept = call(
            functools.partial(middle_kernel, batch),
            [row_out, row_out, spec((rows, model_width), bf16), spec((rows, width), bf16), spec((rows, width), bf16)],
            incoming[batch], cotangent, basis, token_rows, gain, w_gate_up, w_down, *turned,
            scratch=[pltpu.VMEM((rows, model_width), f32), pltpu.VMEM((rows, model_width), f32)],
            flops=8 * rows * coord_width * model_width,
            after=grads[-1:],
        )
        made.append(output)
        grads.append(coord_grad)
        group1 += kept
    arrived = []
    for grad in grads:
        arrived.append(swap_sections(grad))
    group0 = []
    for batch in range(batches):
        (gate_grad,) = call(
            functools.partial(inner_kernel, batch), [spec((rows, width), bf16)],
            arrived[batch], both, turned[1],
            flops=2 * rows * coord_width * width,
            after=group0[-1:],
        )
        group0 += [arrived[batch], gate_grad]
    first_grads = call(
        back_kernel, [row_out] * batches,
        both, expanded, inverse, gain, *turned, *arrived,
        scratch=[pltpu.VMEM((full, coord_width), bf16), pltpu.VMEM((full, model_width), f32)],
        flops=4 * full * coord_width * model_width,
    )
    cuts = cuts_of(share_rows + down_rows * (coord_width // width))
    shapes = [(replicas // 2, cut.stop - cut.start, width) for cut in cuts]
    blocks = call(
        grads_kernel, [spec(shape, kind) for kind in (f32, bf16) for shape in shapes],
        normed_turned, hidden, cotangent, *group0, *group1,
        scratch=[
            pltpu.VMEM((full, width), bf16), pltpu.VMEM((full, width), bf16),
            pltpu.VMEM((full, coord_width), bf16), pltpu.VMEM((hidden_width, coord_width), f32),
            pltpu.VMEM((model_width, full), bf16),
        ],
        flops=2 * full * width * (model_width + coord_width),
        limit=16 << 20,
    )
    swapped = [swap_cores(sent, replicas) for sent in blocks[2:]]
    totals = [kept + sent.astype(f32) for kept, sent in zip(blocks, swapped)]
    for turn in range(turns - 1, -1, -1):
        half = totals[0].shape[0] // 2
        come = []
        for total, kinds in zip(totals, REDUCE):
            come.append(exchange(total[half:].astype(bf16), replicas, turn, kinds))
        totals = [total[:half] for total in totals]
        if turn:
            totals = [total + part.astype(f32) for total, part in zip(totals, come)]
    produced, returned = call(
        select_kernel, [spec((1,) + coords_in.shape, bf16)] * 2, *outputs, *made, *first_grads, *grads
    )
    grad_scale = 1.0 / math.sqrt(full * replicas)
    weights = (gate_weight, gate_moment, gate_second, down_weight, down_moment, down_second)
    updated = call(
        functools.partial(finish_kernel, grad_scale),
        [spec(weight.shape, f32) for weight in weights],
        *totals, *come, *weights,
    )
    return (produced, returned, *updated)


def per_device(
    coords_in,
    token_rows,
    cotangent,
    subspace_basis,
    norm_gain,
    gate_weight,
    up_weight,
    down_weight,
    gate_moment,
    gate_second,
    down_moment,
    down_second,
):
    batches, rows_dev, coord_width = coords_in.shape
    model_width = subspace_basis.shape[1]
    sections = lax.axis_size("section")
    replicas = lax.axis_size("replica")
    section = lax.axis_index("section")
    share_rows, hidden_width = gate_weight.shape[1:]
    down_rows = down_weight.shape[1]
    bf16 = jnp.bfloat16

    gate_up = jnp.concatenate([gate_weight[0].astype(bf16), up_weight[0]], axis=1)
    down = down_weight[0].astype(bf16)
    packed = jnp.concatenate([gate_up, down.reshape(-1, gate_up.shape[1])], axis=0)
    gathered = gather_shares(packed)
    w_gate_up = gathered[:, :share_rows].reshape(model_width, 2 * hidden_width)
    w_down = gathered[:, share_rows:].reshape(hidden_width, coord_width)

    def put(buffer, item, slot):
        return lax.dynamic_update_index_in_dim(buffer, item, slot, 0)

    def get(buffer, slot):
        return lax.dynamic_index_in_dim(buffer, slot, 0, False)

    def room(*dims, kind=bf16):
        return jnp.zeros((batches + 1, rows_dev) + dims, kind)

    store = {
        "output": room(coord_width),
        "expanded": room(model_width, kind=jnp.float32),
        "inverse": room(1, kind=jnp.float32),
        "normed": room(model_width),
        "gate": room(hidden_width, kind=jnp.float32),
        "up": room(hidden_width, kind=jnp.float32),
        "hidden": room(hidden_width),
        "returned": room(coord_width),
        "next_grad": room(coord_width),
        "gate_grad": room(hidden_width),
    }
    blank = jnp.zeros((rows_dev, coord_width), bf16)

    def forward(tick, incoming):
        batch = tick - section
        slot = jnp.clip(batch, 0, batches)
        read = jnp.clip(batch, 0, batches - 1)
        source = jnp.where(section == 0, get(coords_in, read), incoming)
        expanded = jnp.dot(source, subspace_basis, preferred_element_type=jnp.float32) + get(
            token_rows, read
        ).astype(jnp.float32)
        inverse = lax.rsqrt(jnp.mean(expanded * expanded, axis=1, keepdims=True) + epsilon)
        normed = (expanded * inverse * norm_gain).astype(bf16)
        both = jnp.dot(normed, w_gate_up, preferred_element_type=jnp.float32)
        gate, up = both[:, :hidden_width], both[:, hidden_width:]
        hidden = (gate * jax.nn.sigmoid(gate) * up).astype(bf16)
        output = (
            source.astype(jnp.float32)
            + jnp.dot(hidden, w_down, preferred_element_type=jnp.float32)
        ).astype(bf16)
        for name, item in (
            ("output", output),
            ("expanded", expanded),
            ("inverse", inverse),
            ("normed", normed),
            ("gate", gate),
            ("up", up),
            ("hidden", hidden),
        ):
            store[name] = put(store[name], item, slot)
        return shift(output, "section", 1)

    def backward(tick, incoming):
        batch = tick - (sections - 1 - section)
        live = (batch >= 0) & (batch < batches)
        slot = jnp.clip(batch, 0, batches)
        read = jnp.clip(batch, 0, batches - 1)
        next_grad = jnp.where(section == sections - 1, get(cotangent, read), incoming)
        next_grad = jnp.where(live, next_grad, jnp.zeros_like(next_grad))
        gate, up = get(store["gate"], read), get(store["up"], read)
        expanded, inverse = get(store["expanded"], read), get(store["inverse"], read)
        hidden_grad = contract_last(next_grad, w_down)
        sigma = jax.nn.sigmoid(gate)
        gate_grad = (hidden_grad * up * (sigma * (1.0 + gate * (1.0 - sigma)))).astype(bf16)
        up_grad = (hidden_grad * (gate * sigma)).astype(bf16)
        normed_grad = contract_last(jnp.concatenate([gate_grad, up_grad], axis=1), w_gate_up)
        scaled = normed_grad * norm_gain
        centred = expanded * inverse
        expanded_grad = (
            inverse * (scaled - centred * jnp.mean(scaled * centred, axis=1, keepdims=True))
        ).astype(bf16)
        coord_grad = (
            next_grad.astype(jnp.float32) + contract_last(expanded_grad, subspace_basis)
        ).astype(bf16)
        for name, item in (
            ("returned", coord_grad),
            ("next_grad", next_grad),
            ("gate_grad", gate_grad),
        ):
            store[name] = put(store[name], item, slot)
        return shift(coord_grad, "section", -1)

    ticks = sections + batches - 1
    down_stream, up_stream = blank, blank
    for tick in range(ticks + sections - 1):
        if tick < ticks:
            down_stream = forward(tick, down_stream)
        if tick >= sections - 1:
            up_stream = backward(tick - (sections - 1), up_stream)

    def flat(name):
        return store[name][:batches].reshape(batches * rows_dev, -1)

    gate_sum = contract_first(flat("normed"), flat("gate_grad")).astype(bf16)
    down_sum = contract_first(flat("hidden"), flat("next_grad")).astype(bf16)
    down_sum = down_sum.reshape(replicas, down_rows, coord_width)
    pieces = [gate_sum.reshape(replicas, share_rows, hidden_width)]
    for start in range(0, coord_width, hidden_width):
        pieces.append(down_sum[:, :, start : start + hidden_width])
    share = reduce_shares(jnp.concatenate(pieces, axis=1))
    gate_share = share[:share_rows]
    down_share = jnp.concatenate(
        [
            share[start : start + down_rows]
            for start in range(share_rows, share.shape[0], down_rows)
        ],
        axis=1,
    )
    grad_scale = 1.0 / math.sqrt(batches * rows_dev * replicas)
    gate_new, gate_moment_new, gate_second_new = adam_update(
        gate_weight[0], gate_moment[0], gate_second[0], gate_share * grad_scale
    )
    down_new, down_moment_new, down_second_new = adam_update(
        down_weight[0], down_moment[0], down_second[0], down_share * grad_scale
    )
    return (
        store["output"][None, :batches],
        store["returned"][None, :batches],
        gate_new[None],
        gate_moment_new[None],
        gate_second_new[None],
        down_new[None],
        down_moment_new[None],
        down_second_new[None],
    )


def solution(mesh):
    rows = P(None, "replica", None)
    weight = P("section", "replica", None)
    stacked = P("section", None, "replica", None)
    two = mesh.shape["section"] == 2

    def body(*values):
        return (two_sections if two else per_device)(*values)

    return jax.shard_map(
        body,
        mesh=mesh,
        in_specs=(rows, rows, rows, P(), P("section", None)) + (weight,) * 7,
        out_specs=(stacked, stacked) + (weight,) * 6,
        check_vma=False,
    )
```

```python
import functools
import math

import jax
import jax.numpy as jnp
from jax import lax
from jax.experimental import pallas as pl
from jax.experimental.pallas import tpu as pltpu
from jax.sharding import PartitionSpec as P


epsilon = 1e-06
learn_rate = 0.001
decay_first = 0.9
decay_second = 0.95
step_count = 10
adam_floor = 1e-08


def contract_last(left, right):
    return lax.dot_general(
        left, right, (((1,), (1,)), ((), ())), preferred_element_type=jnp.float32
    )


def contract_first(left, right):
    return lax.dot_general(
        left, right, (((0,), (0,)), ((), ())), preferred_element_type=jnp.float32
    )


def shift(value, axis, steps):
    count = lax.axis_size(axis)
    first, last = max(0, -steps), min(count, count - steps)
    return lax.ppermute(value, axis, [(source, source + steps) for source in range(first, last)])


def bit_orders(replicas, kinds="ab"):
    bits = (replicas // 2).bit_length() - 1
    down = list(range(bits - 1, -1, -1))
    known = {"a": down, "b": down[-1:] + down[:-1], "c": down[:1] + down[-1:] + down[1:-1], "d": down[1:-1] + down[:1] + down[-1:]}
    return [known[kind] if bits > 1 else down for kind in kinds]


def exchange(value, replicas, turn, kinds="ab"):
    orders = bit_orders(replicas, kinds)
    pairs = [(r, r ^ (2 << orders[r % 2][turn])) for r in range(replicas)]
    return lax.ppermute(value, "replica", pairs)


def swap_sections(value):
    return lax.ppermute(value, "section", [(0, 1), (1, 0)])


def swap_cores(value, replicas):
    return lax.ppermute(value, "replica", [(r, r ^ 1) for r in range(replicas)])


def offsets(replicas, kinds="ab"):
    tables = []
    for order in bit_orders(replicas, kinds):
        places = [0]
        for bit in order:
            places = places + [place ^ (1 << bit) for place in places]
        tables.append(places)
    return tables


def chip_at(replica, core, table, place):
    return (replica // 2) ^ jnp.where(core == 0, table[0][place], table[1][place])


def gather_shares(share):
    replicas = lax.axis_size("replica")
    replica = lax.axis_index("replica")
    core = replica % 2
    table = offsets(replicas)
    held = share[None]
    for turn in range(len(table[0]).bit_length() - 1):
        held = jnp.concatenate([held, exchange(held, replicas, turn)], axis=0)
    other = swap_cores(held, replicas)
    result = jnp.zeros((replicas,) + share.shape, share.dtype)
    for place in range(replicas // 2):
        mine = chip_at(replica, core, table, place) * 2 + core
        theirs = chip_at(replica, 1 - core, table, place) * 2 + 1 - core
        result = lax.dynamic_update_slice(result, held[place][None], (mine, 0, 0))
        result = lax.dynamic_update_slice(result, other[place][None], (theirs, 0, 0))
    return result


def reduce_shares(partial):
    replicas = lax.axis_size("replica")
    replica = lax.axis_index("replica")
    core = replica % 2
    table = offsets(replicas)
    halves = partial.reshape((replicas // 2, 2) + partial.shape[1:])
    sent = jnp.where(core == 0, halves[:, 1], halves[:, 0])
    kept = jnp.where(core == 0, halves[:, 0], halves[:, 1])
    total = kept.astype(jnp.float32) + swap_cores(sent, replicas).astype(jnp.float32)
    total = jnp.concatenate(
        [
            lax.dynamic_index_in_dim(total, chip_at(replica, core, table, place), 0, True)
            for place in range(replicas // 2)
        ],
        axis=0,
    )
    turns = len(table[0]).bit_length() - 1
    for turn in range(turns - 1, -1, -1):
        half = total.shape[0] // 2
        arrived = exchange(total[half:].astype(jnp.bfloat16), replicas, turn)
        total = total[:half] + arrived.astype(jnp.float32)
    return total[0]


def adam_update(weight_now, moment, second, gradient):
    moment_new = decay_first * moment + (1.0 - decay_first) * gradient
    second_new = decay_second * second + (1.0 - decay_second) * gradient * gradient
    update = (
        learn_rate
        * (moment_new / (1.0 - decay_first**step_count))
        / (jnp.sqrt(second_new / (1.0 - decay_second**step_count)) + adam_floor)
    )
    return (weight_now - update, moment_new, second_new)


WIDE = 512
GATHER = ("ac", "ba")
REDUCE = ("ac", "ac")


def call(kernel, outs, *args, scratch=(), flops=0, limit=12 << 20, after=(), aliases=None):
    moved = sum(math.prod(a.shape) * a.dtype.itemsize for a in args)
    moved += sum(math.prod(o.shape) * o.dtype.itemsize for o in outs)
    spaces = [pltpu.VMEM] * len(args)
    skipped = len(after)
    aliases = {skipped + source: target for source, target in (aliases or {}).items()}

    def body(*refs):
        kernel(*refs[skipped:])

    return pl.pallas_call(
        body,
        out_shape=outs,
        in_specs=[pl.BlockSpec(memory_space=space) for space in [pl.ANY] * skipped + spaces],
        out_specs=[pl.BlockSpec(memory_space=pltpu.VMEM)] * len(outs),
        scratch_shapes=scratch,
        input_output_aliases=aliases,
        compiler_params=pltpu.CompilerParams(vmem_limit_bytes=limit),
        cost_estimate=pl.CostEstimate(flops=flops, bytes_accessed=moved, transcendentals=0),
    )(*after, *args)


def spec(shape, kind):
    return jax.ShapeDtypeStruct(tuple(shape), kind)


def blocks_of(width):
    size = min(WIDE, width)
    return [slice(start, start + size) for start in range(0, width, size)]


def dot(left, right):
    return jnp.dot(left, right, preferred_element_type=jnp.float32)


def near_kernel(value, near):
    near[...] = value[...]


def expand(source, basis, tokens, expanded):
    width = expanded.shape[1]
    squares = 0.0
    for part in blocks_of(width):
        piece = dot(source, basis[:, part]) + tokens[:, part].astype(jnp.float32)
        expanded[:, part] = piece
        squares = squares + jnp.sum(piece * piece, axis=1, keepdims=True)
    return lax.rsqrt(squares * (1.0 / width) + epsilon)


def expand_kernel(source, basis, tokens, gain, expanded, normed, inverse):
    inv = expand(source[...], basis, tokens, expanded)
    inverse[...] = jnp.broadcast_to(inv, inverse.shape)
    for part in blocks_of(normed.shape[1]):
        normed[:, part] = (expanded[:, part] * inv * gain[:, part]).astype(jnp.bfloat16)


def act(both):
    width = both.shape[1] // 2
    gate, up = both[:, :width], both[:, width:]
    sigma = jax.nn.sigmoid(gate)
    return gate, up, sigma


def front(source, normed, w_gate_up, w_down):
    both = 0.0
    for part in blocks_of(normed.shape[1]):
        both = both + dot(normed[:, part], w_gate_up[part, :])
    gate, up, sigma = act(both)
    hidden = (gate * sigma * up).astype(jnp.bfloat16)
    output = (source.astype(jnp.float32) + dot(hidden, w_down[...])).astype(jnp.bfloat16)
    return both, hidden, output


def assemble(pieces, places, first, theirs, w_gate_up, w_down):
    rows = w_gate_up.shape[0] // (2 * places)
    extra = w_down.shape[0] // (2 * places)
    width = w_gate_up.shape[1] // 2
    up, packed = pieces
    for stream in range(2):
        targets = places_of(places, GATHER[stream])[places if theirs else 0 :]
        for place in range(up.shape[0]):
            target = targets[first + place]
            lines = pl.ds(pl.multiple_of(target * rows, rows), rows)
            if stream == 0:
                w_gate_up[lines, width:] = up[place]
                continue
            w_gate_up[lines, :width] = packed[place, :rows, :]
            lines = pl.ds(pl.multiple_of(target * extra, extra), extra)
            for turn, low in enumerate(range(rows, packed.shape[1], extra)):
                w_down[lines, turn * width : (turn + 1) * width] = packed[place, low : low + extra, :]


def early_kernel(*refs):
    *pieces, w_gate_up, w_down = refs
    half = pieces[0].shape[0]
    for index, theirs in enumerate((False, True)):
        assemble(pieces[2 * index : 2 * index + 2], 2 * half, 0, theirs, w_gate_up, w_down)


def own_kernel(up, packed, part_gate_up, part_down, w_gate_up, w_down):
    half = up.shape[0]
    assemble((up, packed), 2 * half, half, False, w_gate_up, w_down)


def front_kernel(up, packed, part_gate_up, part_down, normed, source, w_gate_up, w_down, both, hidden, *outputs):
    half = up.shape[0]
    assemble((up, packed), 2 * half, half, True, w_gate_up, w_down)
    count = source.shape[0] // len(outputs)

    @pl.when(lax.axis_index("section") == 0)
    def _():
        both[...], hidden[...], output = front(source[...], normed, w_gate_up, w_down)
        for index, out in enumerate(outputs):
            out[...] = output[index * count : (index + 1) * count]


def turn_kernel(*refs):
    half = len(refs) // 2
    for source, target in zip(refs[:half], refs[half:]):
        step = min(WIDE, source.shape[0])
        for low in range(0, source.shape[0], step):
            target[:, low : low + step] = source[low : low + step, :].T


def inner(next_grad, both, down_turned):
    gate, up, sigma = act(both)
    hidden_grad = dot(next_grad, down_turned[...])
    gate_grad = (hidden_grad * up * (sigma * (1.0 + gate * (1.0 - sigma)))).astype(jnp.bfloat16)
    up_grad = (hidden_grad * (gate * sigma)).astype(jnp.bfloat16)
    return gate_grad, up_grad


def back(next_grad, both, expanded, inv, gain, gate_up_turned, down_turned, basis_turned, scaled):
    gate_grad, up_grad = inner(next_grad, both, down_turned)
    grads = jnp.concatenate([gate_grad, up_grad], axis=1)
    width = expanded.shape[1]
    total = 0.0
    for part in blocks_of(width):
        piece = dot(grads, gate_up_turned[:, part]) * gain[:, part]
        scaled[:, part] = piece
        total = total + jnp.sum(piece * expanded[:, part], axis=1, keepdims=True)
    mean = total * inv * (1.0 / width)
    coord_grad = next_grad.astype(jnp.float32)
    for part in blocks_of(width):
        piece = inv * (scaled[:, part] - expanded[:, part] * inv * mean)
        coord_grad = coord_grad + dot(piece.astype(jnp.bfloat16), basis_turned[part, :])
    return gate_grad, coord_grad.astype(jnp.bfloat16)


def middle_kernel(
    batch, source, cotangent, basis, tokens, gain, w_gate_up, w_down,
    gate_up_turned, down_turned, basis_turned, output, coord_grad, normed, hidden, gate_grad, expanded, scaled,
):
    cot, tokens = cotangent.at[batch], tokens.at[batch]

    @pl.when(lax.axis_index("section") != 0)
    def _():
        start = source[...]
        inv = expand(start, basis, tokens, expanded)
        for part in blocks_of(normed.shape[1]):
            normed[:, part] = (expanded[:, part] * inv * gain[:, part]).astype(jnp.bfloat16)
        both, hidden[...], output[...] = front(start, normed, w_gate_up, w_down)
        gate_grad[...], coord_grad[...] = back(
            cot[...], both, expanded, inv, gain, gate_up_turned, down_turned, basis_turned, scaled
        )


def inner_kernel(batch, next_grad, both, down_turned, gate_grad):
    rows = pl.ds(batch * next_grad.shape[0], next_grad.shape[0])

    @pl.when(lax.axis_index("section") == 0)
    def _():
        gate_grad[...] = inner(next_grad[...], both[rows, :], down_turned)[0]


def back_kernel(*refs):
    both, expanded, inverse, gain, gate_up_turned, down_turned, basis_turned, *refs = refs
    *values, next_grad, scaled = refs
    half = len(values) // 2

    @pl.when(lax.axis_index("section") == 0)
    def _():
        count = values[0].shape[0]
        for batch in range(half):
            next_grad[pl.ds(batch * count, count), :] = values[batch][...]
        coord_grad = back(
            next_grad[...], both[...], expanded, inverse[:, :1],
            gain, gate_up_turned, down_turned, basis_turned, scaled,
        )[1]
        for batch in range(half):
            values[half + batch][...] = coord_grad[batch * count : (batch + 1) * count]


def grads_kernel(theirs, *refs):
    *inputs, block_a, block_b, hidden, gate_grad, next_grad, down_all, turned = refs
    turned0, hidden0, cotangent, *inputs = inputs
    batches, count, _ = cotangent.shape
    places, _, width = block_a.shape
    section = lax.axis_index("section")

    @pl.when(section == 0)
    def _():
        hidden[...] = hidden0[...]
        for batch in range(batches):
            rows = pl.ds(batch * count, count)
            next_grad[rows, :] = inputs[2 * batch][...]
            gate_grad[rows, :] = inputs[2 * batch + 1][...]

    @pl.when(section != 0)
    def _():
        for batch in range(batches):
            rows = pl.ds(batch * count, count)
            group = inputs[2 * batches + 3 * batch : 2 * batches + 3 * batch + 3]
            next_grad[rows, :] = cotangent[batch]
            hidden[rows, :] = group[1][...]
            gate_grad[rows, :] = group[2][...]
            for part in blocks_of(turned.shape[0]):
                turned[part, rows] = group[0][:, part].T

    down_all[...] = contract_first(hidden[...], next_grad[...])
    rows = turned.shape[0] // (2 * places)
    extra = down_all.shape[0] // (2 * places)
    cuts = cuts_of(rows + extra * (down_all.shape[1] // width))

    def fill(source):
        targets = places_of(places, REDUCE[0])
        for place, target in enumerate(targets[places:] if theirs else targets[:places]):
            lines = down_all[pl.ds(pl.multiple_of(target * extra, extra), extra), :]
            gate = dot(source[pl.ds(pl.multiple_of(target * rows, rows), rows), :], gate_grad[...])
            for cut, block in zip(cuts, (block_a, block_b)):
                top = min(cut.stop, rows)
                block[place, : top - cut.start, :] = gate[cut.start : top, :].astype(block.dtype)
                if cut.stop > rows:
                    for turn in range(lines.shape[1] // width):
                        low = top - cut.start + turn * extra
                        block[place, low : low + extra, :] = lines[
                            :, turn * width : (turn + 1) * width
                        ].astype(block.dtype)

    @pl.when(section == 0)
    def _():
        fill(turned0)

    @pl.when(section != 0)
    def _():
        fill(turned)


def cuts_of(rows):
    first = rows // 32 * 16
    return [slice(0, first), slice(first, rows)]


def places_of(places, kinds):
    replica = lax.axis_index("replica")
    core, chip = replica & 1, replica >> 1
    table = offsets(2 * places, kinds)
    result = []
    for which in (core, 1 - core):
        for low, high in zip(*table):
            result.append((chip ^ jnp.where(which == 0, low, high)) * 2 + which)
    return result


def select_kernel(*refs):
    *inputs, produced, returned = refs
    batches = produced.shape[1]
    section = lax.axis_index("section")
    for index, target in enumerate((produced, returned)):
        for batch in range(batches):
            first = inputs[2 * batches * index + batch]
            second = inputs[2 * batches * index + batches + batch]

            @pl.when(section == 0)
            def _(first=first, target=target, batch=batch):
                target[0, batch] = first[...]

            @pl.when(section != 0)
            def _(second=second, target=target, batch=batch):
                target[0, batch] = second[...]


def finish_kernel(scale, *refs):
    kept_a, kept_b, come_a, come_b, gw, gm, gs, dw, dm, ds, *outs = refs
    rows = gw.shape[1]
    extra = dw.shape[1]
    parts = [kept[0] + come[0].astype(jnp.float32) for kept, come in ((kept_a, come_a), (kept_b, come_b))]
    share = jnp.concatenate(parts, axis=0) * scale
    gate = share[:rows]
    down = jnp.concatenate(
        [share[low : low + extra] for low in range(rows, share.shape[0], extra)], axis=1
    )
    for values, grad, targets in (((gw, gm, gs), gate, outs[:3]), ((dw, dm, ds), down, outs[3:])):
        results = adam_update(*(value[0] for value in values), grad)
        for target, result in zip(targets, results):
            target[0] = result


def two_sections(
    coords_in, token_rows, cotangent, basis, gain, gate_weight, up_weight, down_weight,
    gate_moment, gate_second, down_moment, down_second,
):
    batches, rows, coord_width = coords_in.shape
    model_width = basis.shape[1]
    replicas = lax.axis_size("replica")
    share_rows, width = gate_weight.shape[1:]
    down_rows = down_weight.shape[1]
    bf16, f32 = jnp.bfloat16, jnp.float32
    hidden_width = down_rows * replicas
    full = batches * rows
    lines = [down_weight[0, :, low : low + width] for low in range(0, coord_width, width)]
    packed = jnp.concatenate([part.astype(bf16) for part in (gate_weight[0], *lines)], axis=0)
    (up_near,) = call(near_kernel, [spec(up_weight.shape, bf16)], up_weight)
    held = [up_near, packed[None]]
    turns = (replicas // 2).bit_length() - 1
    source = coords_in.reshape(full, coord_width)
    tokens = token_rows.reshape(full, model_width)
    expanded, normed, inverse = call(
        expand_kernel,
        [spec((full, model_width), f32), spec((full, model_width), bf16), spec((full, 128), f32)],
        source, basis, tokens, gain,
        flops=2 * full * coord_width * model_width,
    )
    for turn in range(turns):
        come = []
        for part, kinds, name in zip(held, GATHER, ("up", "packed")):
            sent = up_weight if turn == 0 and name == "up" else part
            come.append(exchange(sent, replicas, turn, kinds))
        if turn < turns - 1:
            held = [jnp.concatenate(pair, axis=0) for pair in zip(held, come)]
    theirs = []
    for part, name in zip(held, ("up", "packed")):
        theirs.append(swap_cores(part, replicas))
    last = [swap_cores(part, replicas) for part in come]
    weights = [spec((model_width, 2 * width), bf16), spec((hidden_width, coord_width), bf16)]
    parts = call(early_kernel, weights, *held, *theirs)
    part_gate_up, part_down = call(own_kernel, weights, *come, *parts, aliases={2: 0, 3: 1})
    row_out = spec((rows, coord_width), bf16)
    w_gate_up, w_down, both, hidden, *outputs = call(
        front_kernel,
        weights + [spec((full, 2 * width), f32), spec((full, width), bf16)] + [row_out] * batches,
        *last, part_gate_up, part_down, normed, source,
        flops=4 * full * width * model_width,
        aliases={2: 0, 3: 1},
    )
    incoming = [swap_sections(outputs[0])]
    turned = call(
        turn_kernel,
        [spec(value.shape[::-1], bf16) for value in (w_gate_up, w_down, basis, normed)],
        w_gate_up, w_down, basis, normed,
        limit=16 << 20,
    )
    later, turned = lax.optimization_barrier((outputs[1:], turned))
    incoming += [swap_sections(out) for out in later]
    *turned, normed_turned = turned
    made, grads, group1 = [], [], []
    for batch in range(batches):
        output, coord_grad, *kept = call(
            functools.partial(middle_kernel, batch),
            [row_out, row_out, spec((rows, model_width), bf16), spec((rows, width), bf16), spec((rows, width), bf16)],
            incoming[batch], cotangent, basis, token_rows, gain, w_gate_up, w_down, *turned,
            scratch=[pltpu.VMEM((rows, model_width), f32), pltpu.VMEM((rows, model_width), f32)],
            flops=8 * rows * coord_width * model_width,
            after=grads[-1:],
        )
        made.append(output)
        grads.append(coord_grad)
        group1 += kept
    arrived = []
    for grad in grads:
        arrived.append(swap_sections(grad))
    group0 = []
    for batch in range(batches):
        (gate_grad,) = call(
            functools.partial(inner_kernel, batch), [spec((rows, width), bf16)],
            arrived[batch], both, turned[1],
            flops=2 * rows * coord_width * width,
            after=group0[-1:],
        )
        group0 += [arrived[batch], gate_grad]
    first_grads = call(
        back_kernel, [row_out] * batches,
        both, expanded, inverse, gain, *turned, *arrived,
        scratch=[pltpu.VMEM((full, coord_width), bf16), pltpu.VMEM((full, model_width), f32)],
        flops=4 * full * coord_width * model_width,
    )
    cuts = cuts_of(share_rows + down_rows * (coord_width // width))
    shapes = [(replicas // 2, cut.stop - cut.start, width) for cut in cuts]

    def blocks_for(theirs):
        return call(
            functools.partial(grads_kernel, theirs), [spec(shape, bf16 if theirs else f32) for shape in shapes],
            normed_turned, hidden, cotangent, *group0, *group1,
            scratch=[
                pltpu.VMEM((full, width), bf16), pltpu.VMEM((full, width), bf16),
                pltpu.VMEM((full, coord_width), bf16), pltpu.VMEM((hidden_width, coord_width), f32),
                pltpu.VMEM((model_width, full), bf16),
            ],
            flops=full * width * (model_width + coord_width),
            limit=16 << 20,
        )

    swapped = []
    for sent in blocks_for(True):
        swapped.append(swap_cores(sent, replicas))
    kept = blocks_for(False)
    totals = [own + sent.astype(f32) for own, sent in zip(kept, swapped)]
    for turn in range(turns - 1, -1, -1):
        half = totals[0].shape[0] // 2
        come = []
        for total, kinds in zip(totals, REDUCE):
            come.append(exchange(total[half:].astype(bf16), replicas, turn, kinds))
        totals = [total[:half] for total in totals]
        if turn:
            totals = [total + part.astype(f32) for total, part in zip(totals, come)]
    produced, returned = call(
        select_kernel, [spec((1,) + coords_in.shape, bf16)] * 2, *outputs, *made, *first_grads, *grads
    )
    grad_scale = 1.0 / math.sqrt(full * replicas)
    weights = (gate_weight, gate_moment, gate_second, down_weight, down_moment, down_second)
    updated = call(
        functools.partial(finish_kernel, grad_scale),
        [spec(weight.shape, f32) for weight in weights],
        *totals, *come, *weights,
    )
    return (produced, returned, *updated)


def per_device(
    coords_in,
    token_rows,
    cotangent,
    subspace_basis,
    norm_gain,
    gate_weight,
    up_weight,
    down_weight,
    gate_moment,
    gate_second,
    down_moment,
    down_second,
):
    batches, rows_dev, coord_width = coords_in.shape
    model_width = subspace_basis.shape[1]
    sections = lax.axis_size("section")
    replicas = lax.axis_size("replica")
    section = lax.axis_index("section")
    share_rows, hidden_width = gate_weight.shape[1:]
    down_rows = down_weight.shape[1]
    bf16 = jnp.bfloat16

    gate_up = jnp.concatenate([gate_weight[0].astype(bf16), up_weight[0]], axis=1)
    down = down_weight[0].astype(bf16)
    packed = jnp.concatenate([gate_up, down.reshape(-1, gate_up.shape[1])], axis=0)
    gathered = gather_shares(packed)
    w_gate_up = gathered[:, :share_rows].reshape(model_width, 2 * hidden_width)
    w_down = gathered[:, share_rows:].reshape(hidden_width, coord_width)

    def put(buffer, item, slot):
        return lax.dynamic_update_index_in_dim(buffer, item, slot, 0)

    def get(buffer, slot):
        return lax.dynamic_index_in_dim(buffer, slot, 0, False)

    def room(*dims, kind=bf16):
        return jnp.zeros((batches + 1, rows_dev) + dims, kind)

    store = {
        "output": room(coord_width),
        "expanded": room(model_width, kind=jnp.float32),
        "inverse": room(1, kind=jnp.float32),
        "normed": room(model_width),
        "gate": room(hidden_width, kind=jnp.float32),
        "up": room(hidden_width, kind=jnp.float32),
        "hidden": room(hidden_width),
        "returned": room(coord_width),
        "next_grad": room(coord_width),
        "gate_grad": room(hidden_width),
    }
    blank = jnp.zeros((rows_dev, coord_width), bf16)

    def forward(tick, incoming):
        batch = tick - section
        slot = jnp.clip(batch, 0, batches)
        read = jnp.clip(batch, 0, batches - 1)
        source = jnp.where(section == 0, get(coords_in, read), incoming)
        expanded = jnp.dot(source, subspace_basis, preferred_element_type=jnp.float32) + get(
            token_rows, read
        ).astype(jnp.float32)
        inverse = lax.rsqrt(jnp.mean(expanded * expanded, axis=1, keepdims=True) + epsilon)
        normed = (expanded * inverse * norm_gain).astype(bf16)
        both = jnp.dot(normed, w_gate_up, preferred_element_type=jnp.float32)
        gate, up = both[:, :hidden_width], both[:, hidden_width:]
        hidden = (gate * jax.nn.sigmoid(gate) * up).astype(bf16)
        output = (
            source.astype(jnp.float32)
            + jnp.dot(hidden, w_down, preferred_element_type=jnp.float32)
        ).astype(bf16)
        for name, item in (
            ("output", output),
            ("expanded", expanded),
            ("inverse", inverse),
            ("normed", normed),
            ("gate", gate),
            ("up", up),
            ("hidden", hidden),
        ):
            store[name] = put(store[name], item, slot)
        return shift(output, "section", 1)

    def backward(tick, incoming):
        batch = tick - (sections - 1 - section)
        live = (batch >= 0) & (batch < batches)
        slot = jnp.clip(batch, 0, batches)
        read = jnp.clip(batch, 0, batches - 1)
        next_grad = jnp.where(section == sections - 1, get(cotangent, read), incoming)
        next_grad = jnp.where(live, next_grad, jnp.zeros_like(next_grad))
        gate, up = get(store["gate"], read), get(store["up"], read)
        expanded, inverse = get(store["expanded"], read), get(store["inverse"], read)
        hidden_grad = contract_last(next_grad, w_down)
        sigma = jax.nn.sigmoid(gate)
        gate_grad = (hidden_grad * up * (sigma * (1.0 + gate * (1.0 - sigma)))).astype(bf16)
        up_grad = (hidden_grad * (gate * sigma)).astype(bf16)
        normed_grad = contract_last(jnp.concatenate([gate_grad, up_grad], axis=1), w_gate_up)
        scaled = normed_grad * norm_gain
        centred = expanded * inverse
        expanded_grad = (
            inverse * (scaled - centred * jnp.mean(scaled * centred, axis=1, keepdims=True))
        ).astype(bf16)
        coord_grad = (
            next_grad.astype(jnp.float32) + contract_last(expanded_grad, subspace_basis)
        ).astype(bf16)
        for name, item in (
            ("returned", coord_grad),
            ("next_grad", next_grad),
            ("gate_grad", gate_grad),
        ):
            store[name] = put(store[name], item, slot)
        return shift(coord_grad, "section", -1)

    ticks = sections + batches - 1
    down_stream, up_stream = blank, blank
    for tick in range(ticks + sections - 1):
        if tick < ticks:
            down_stream = forward(tick, down_stream)
        if tick >= sections - 1:
            up_stream = backward(tick - (sections - 1), up_stream)

    def flat(name):
        return store[name][:batches].reshape(batches * rows_dev, -1)

    gate_sum = contract_first(flat("normed"), flat("gate_grad")).astype(bf16)
    down_sum = contract_first(flat("hidden"), flat("next_grad")).astype(bf16)
    down_sum = down_sum.reshape(replicas, down_rows, coord_width)
    pieces = [gate_sum.reshape(replicas, share_rows, hidden_width)]
    for start in range(0, coord_width, hidden_width):
        pieces.append(down_sum[:, :, start : start + hidden_width])
    share = reduce_shares(jnp.concatenate(pieces, axis=1))
    gate_share = share[:share_rows]
    down_share = jnp.concatenate(
        [
            share[start : start + down_rows]
            for start in range(share_rows, share.shape[0], down_rows)
        ],
        axis=1,
    )
    grad_scale = 1.0 / math.sqrt(batches * rows_dev * replicas)
    gate_new, gate_moment_new, gate_second_new = adam_update(
        gate_weight[0], gate_moment[0], gate_second[0], gate_share * grad_scale
    )
    down_new, down_moment_new, down_second_new = adam_update(
        down_weight[0], down_moment[0], down_second[0], down_share * grad_scale
    )
    return (
        store["output"][None, :batches],
        store["returned"][None, :batches],
        gate_new[None],
        gate_moment_new[None],
        gate_second_new[None],
        down_new[None],
        down_moment_new[None],
        down_second_new[None],
    )


def solution(mesh):
    rows = P(None, "replica", None)
    weight = P("section", "replica", None)
    stacked = P("section", None, "replica", None)
    two = mesh.shape["section"] == 2

    def body(*values):
        return (two_sections if two else per_device)(*values)

    return jax.shard_map(
        body,
        mesh=mesh,
        in_specs=(rows, rows, rows, P(), P("section", None)) + (weight,) * 7,
        out_specs=(stacked, stacked) + (weight,) * 6,
        check_vma=False,
    )
```
